512 devices in a mesh: depth: 8 (over z_hi, core), scan: 64 (over z_lo, y, x).
Axes of the slice: x: 4, y: 4, z: 16 (z_hi: 4, z_lo: 4; z = z_hi * 4 + z_lo), core: 2. Of those that a mesh axis runs over, the one named last changes fastest.
Arguments:
- objects: float32 [24, 2, 8192, 256], P('depth', None, 'scan')
- probe: float32 [2, 128, 128], replicated, may hold values from -6 to 6
- row_offsets: int32 [128], P('scan'), may hold values from 0 to 8192, as said below
- col_offsets: int32 [128], P('scan'), may hold values from 0 to 128, as said below
- intensity: float32 [128, 128, 128], P('scan'), may hold values from 0.1 to 4
Outputs:
- object_grad: float32 [24, 2, 8192, 256], P('depth', None, 'scan')
- probe_grad: float32 [2, 128, 128], P(None, 'depth')
The draws below stay inside these ranges and needn't reach their ends.
Inputs may be any that keep to these rules, and one draw needn't show every extreme that they name: `row_offsets`: position i is measured by scan index i // 2; its row offset lies from (i // 2) * 128 to (i // 2 + 1) * 128, both ends included, and on every scan index one of its positions has the upper end. `col_offsets`: some position has column offset 0 and some has the largest.
All inputs are finite; a program needn't handle non-finite values.
Results may differ from the reference program's by a relative error of at most 0.0003.
Values sent between devices are 32-bit elements; how exact they have to be, the bound alone decides.
A program may use at most 64 MiB of HBM per device.

```python
import math
import jax
import jax.numpy as jnp
from jax import lax

WIN = 128
WAVES = 2
TILE_R = 128
OBJ_COLS = 256
SLICES = 24
OBJ_ROWS = 8192
POSITIONS = 128


def draw_objects(key, part):
    key_amp, key_phase = jax.random.split(jax.random.fold_in(key, 11))
    plane_shape = (SLICES, OBJ_ROWS, OBJ_COLS)
    amplitude = jax.random.uniform(key_amp, plane_shape, jnp.float32, 0.8, 1.2)
    phase_value = jax.random.uniform(key_phase, plane_shape, jnp.float32, -math.pi, math.pi)
    return jnp.stack([amplitude * jnp.cos(phase_value), amplitude * jnp.sin(phase_value)], axis=1)


def draw_row_offsets(key, part):
    key_local, key_pick = jax.random.split(jax.random.fold_in(key, 23))
    local_rows = jax.random.randint(key_local, (POSITIONS,), 0, TILE_R + 1, jnp.int32)
    owner = jnp.arange(POSITIONS, dtype=jnp.int32) // WAVES
    picked = jax.random.randint(key_pick, (POSITIONS // WAVES,), 0, WAVES, jnp.int32)
    forced = jnp.arange(POSITIONS, dtype=jnp.int32) % WAVES == picked[owner]
    local_rows = jnp.where(forced, TILE_R, local_rows)
    return owner * TILE_R + local_rows


def draw_col_offsets(key, part):
    key_cols, key_perm = jax.random.split(jax.random.fold_in(key, 37))
    columns = jax.random.randint(key_cols, (POSITIONS,), 0, OBJ_COLS - WIN + 1, jnp.int32)
    order = jax.random.permutation(key_perm, POSITIONS)
    columns = columns.at[order[0]].set(OBJ_COLS - WIN)
    columns = columns.at[order[1]].set(0)
    return columns


def block_levels(stream_key, extent, shards, least, largest):
    def one(dim, shards_of):
        draws = jax.random.uniform(jax.random.fold_in(jax.random.fold_in(stream_key, 6), dim), (shards_of,), jnp.float32, least / len(shards), largest / len(shards))
        return jnp.repeat(jnp.exp(draws), extent[dim] // shards_of).reshape((-1,) + (1,) * (len(extent) - dim - 1))

    gain = one(*shards[0])
    for cut in shards[1:]:
        gain = gain * one(*cut)
    return gain


def gaussian(key, shape, spread, most, held_as=jnp.bfloat16):
    return jnp.clip(spread * jax.random.normal(key, shape, jnp.float32), -most, most).astype(held_as)


def setup_inputs(seed: int = 0) -> dict:
    key_of = jax.random.split(jax.random.key(seed), 6)
    return {
        "objects": draw_objects(jax.random.fold_in(key_of[5], 71), 0),
        "probe": gaussian(key_of[1], (2, WIN, WIN), 1.0, 6.0, jnp.float32),
        "row_offsets": draw_row_offsets(jax.random.fold_in(key_of[5], 71), 0),
        "col_offsets": draw_col_offsets(jax.random.fold_in(key_of[5], 71), 0),
        "intensity": jnp.clip(jnp.exp(math.log(4.0) - 3.6888794 * jax.random.uniform(key_of[4], (POSITIONS, WIN, WIN), jnp.float32) ** block_levels(key_of[4], (POSITIONS, WIN, WIN), ((0, 64),), -0.2, 0.2)), 0.1, 4.0),
    }


PROPAGATION = 0.5


def reference(objects, probe, row_offsets, col_offsets, intensity):
    slab_total = objects.shape[0]
    object_rows = objects.shape[2]
    window_width = probe.shape[-1]
    extended = jnp.concatenate([objects, objects[:, :, :window_width, :]], axis=2)
    grid_index = jnp.arange(window_width, dtype=jnp.int32)
    frequency = jnp.where(grid_index < window_width // 2, grid_index, grid_index - window_width)
    squared = frequency[:, None] ** 2 + frequency[None, :] ** 2
    phase_angle = squared.astype(probe.dtype) * (PROPAGATION * math.pi / window_width)
    factor = lax.complex(jnp.cos(phase_angle), -jnp.sin(phase_angle))
    start_wave = lax.complex(probe[0], probe[1])
    window_shape = (slab_total, 2, window_width, window_width)

    def forward_fft(values):
        return jnp.fft.fft2(values, norm="ortho")

    def inverse_fft(values):
        return jnp.fft.ifft2(values, norm="ortho")

    def one_position(loop_state, position):
        accum, probe_sum = loop_state
        row_start, col_start, measured = position
        corner = (jnp.int32(0), jnp.int32(0), row_start.astype(jnp.int32), col_start.astype(jnp.int32))
        window = lax.dynamic_slice(extended, corner, window_shape)
        layers = lax.complex(window[:, 0], window[:, 1])

        def forward(wave, layer_now):
            return inverse_fft(factor * forward_fft(wave * layer_now)), wave

        exit_wave, inputs = lax.scan(forward, start_wave, layers)
        far_wave = forward_fft(exit_wave)
        misfit = far_wave.real ** 2 + far_wave.imag ** 2 - measured
        back_start = inverse_fft(2.0 * misfit * far_wave)

        def backward(gradient, pair):
            layer_now, wave_in = pair
            chi_grad = inverse_fft(jnp.conj(factor) * forward_fft(gradient))
            return jnp.conj(layer_now) * chi_grad, jnp.conj(wave_in) * chi_grad

        first_grad, layer_grads = lax.scan(backward, back_start, (layers, inputs), reverse=True)
        update = jnp.stack([layer_grads.real, layer_grads.imag], axis=1)
        accum = lax.dynamic_update_slice(accum, lax.dynamic_slice(accum, corner, window_shape) + update, corner)
        return (accum, probe_sum + first_grad), None

    accum_start = jnp.zeros(extended.shape, objects.dtype)
    probe_start = lax.complex(jnp.zeros_like(probe[0]), jnp.zeros_like(probe[0]))
    (accum, probe_sum), unused = lax.scan(one_position, (accum_start, probe_start), (row_offsets, col_offsets, intensity))
    object_grad = accum[:, :, :object_rows, :].at[:, :, :window_width, :].add(accum[:, :, object_rows:, :])
    probe_grad = jnp.stack([probe_sum.real, probe_sum.imag])
    return object_grad, probe_grad
```

```python
import jax
import jax.numpy as jnp
import ml_dtypes
import numpy as np
from jax import lax
from jax.experimental import pallas as pl
from jax.experimental.pallas import tpu as pltpu
from jax.sharding import PartitionSpec as P

PROPAGATION = 0.5
F32 = jnp.float32
BF16 = jnp.bfloat16
MESH = pl.DeviceIdType.MESH


def split_table(table):
    high = table.astype(ml_dtypes.bfloat16)
    low = (table - high.astype(np.float64)).astype(ml_dtypes.bfloat16)
    return high, low


def block_tables(matrix):
    real, imag = matrix.real, matrix.imag
    right_high, right_low = split_table(np.block([[real, imag], [-imag, real]]))
    left_high, left_low = split_table(np.block([[real, -imag], [imag, real]]))
    return np.concatenate([right_high, right_high, right_low], 0), left_high, left_low


def transfer_tables(width):
    index = np.arange(width)
    frequency = np.where(index < width // 2, index, index - width).astype(np.float64)
    fourier = np.exp(-2j * np.pi * (np.outer(index, index) % width) / width) / np.sqrt(width)
    chirp = np.exp(-1j * PROPAGATION * np.pi * frequency**2 / width)
    spread = fourier.conj() @ (chirp[:, None] * fourier)
    return block_tables(spread) + block_tables(fourier)


def grid_of(count):
    sides = []
    while count > 1:
        side = 4 if count % 4 == 0 else 2 if count % 2 == 0 else count
        sides.insert(0, side)
        count //= side
    return sides


def split(x):
    high = x.astype(BF16)
    return high, (x - high.astype(F32)).astype(BF16)


def dot(a, b):
    return jnp.dot(a, b, preferred_element_type=F32)


def both_sides(real, imag, right, left_high, left_low):
    width = real.shape[0]
    high, low = split(jnp.concatenate([real, imag], 1))
    mid = dot(jnp.concatenate([high, low, high], 1), right[...])
    high, low = split(jnp.concatenate([mid[:, :width], mid[:, width:]], 0))
    pair = dot(left_high[...], jnp.concatenate([high, low], 1))
    out = pair[:, :width] + pair[:, width:] + dot(left_low[...], high)
    return out[:width], out[width:]


def make_kernel(depth_count, scan_count, slab, width):
    stages = depth_count // 2
    count = 2 * slab
    sides = grid_of(scan_count)

    def kernel(
        scal, objects, probe, intensity, right, left_high, left_low, dft_right, dft_left_high, dft_left_low,
        grad, probe_grad,
        halo_out, pair_out, own_win, halo_win, ext, win, waves, back_in, back, steps, canvas,
        mine, pair_send, pair_in, spill_out, spill_in, seen_out, seen_in, chunks, parts, total, around,
        send_halo, send_pair, send_wave, send_back, send_grad, send_spill, send_seen, send_chunk, send_around,
        recv_halo, recv_pair, recv_wave, recv_back, recv_grad, recv_spill, recv_seen, recv_chunk, recv_around,
    ):
        dep = lax.axis_index("depth")
        me = lax.axis_index("scan")
        stage = dep // 2
        core = dep % 2
        first = stage == 0
        last = stage == stages - 1
        split_core = core == 0
        after = lax.rem(me + 1, scan_count)
        before = lax.rem(me + scan_count - 1, scan_count)
        partner = (dep + 1 - 2 * core, me)
        crew = [((lax.rem(dep + k, depth_count)), me) for k in range(1, depth_count)]
        cliques = []
        stride = scan_count
        for side in sides:
            stride //= side
            place = (me // stride) % side
            cliques.append(
                [(dep, me + (lax.rem(place + k, side) - place) * stride) for k in range(1, side)]
            )
        friends = crew + [(2 * stage + k, near) for near in (after, before) for k in range(2)]
        for clique in cliques:
            friends = friends + clique

        def copy(source, target, send, recv, device):
            return pltpu.make_async_remote_copy(
                src_ref=source, dst_ref=target, send_sem=send, recv_sem=recv,
                device_id=device, device_id_type=MESH,
            )

        barrier = pltpu.get_barrier_semaphore()
        for friend in friends:
            pl.semaphore_signal(barrier, inc=1, device_id=friend, device_id_type=MESH)
        pl.semaphore_wait(barrier, len(friends))

        col_split, row_split, col_whole, col_before, whole_is_second = [scal[k] for k in range(5)]
        col_mine = jnp.where(split_core, col_split, col_whole)
        col_pair = jnp.where(split_core, col_whole, col_split)
        rows = jnp.where(split_core, row_split, 0)

        def halo_copy(k):
            return copy(
                halo_out.at[k], halo_win.at[slab * core + k], send_halo.at[k],
                recv_halo.at[slab * core + k], (2 * stage, before),
            )

        def pair_copy(k):
            return copy(
                pair_out.at[k], own_win.at[slab * core + k], send_pair.at[k], recv_pair.at[k], partner
            )

        def seen_copy():
            return copy(seen_out, seen_in, send_seen, recv_seen, (dep, after))

        def wave_copy():
            return copy(waves.at[count], waves.at[0], send_wave, recv_wave, (dep + 2, me))

        def back_copy():
            return copy(back, back_in, send_back, recv_back, (dep - 2, me))

        def grad_copy(k):
            return copy(pair_send.at[k], pair_in.at[k], send_grad.at[k], recv_grad.at[k], partner)

        def spill_copy(k):
            return copy(
                spill_out.at[k], spill_in.at[k % slab], send_spill.at[k], recv_spill.at[k % slab],
                (2 * stage + k // slab, after),
            )

        def chunk_copy(k):
            target = lax.rem(dep + k, depth_count)
            return copy(
                chunks.at[target], parts.at[core], send_chunk.at[k], recv_chunk.at[core], (target, me)
            )

        def shifted_left(plane, amount):
            return pltpu.roll(plane, lax.rem(2 * width - amount, 2 * width), 1)[:, :width]

        for k in range(slab):
            for part in range(2):
                plane = objects[k, part]
                halo_out[k, part] = shifted_left(plane, col_before)
                pair_out[k, part] = shifted_left(plane, col_pair)
                own_win[slab * core + k, part] = shifted_left(plane, col_mine)
            halo_copy(k).start()
            pair_copy(k).start()

        measured_split = jnp.where(whole_is_second == 1, intensity[0], intensity[1])
        measured_whole = jnp.where(whole_is_second == 1, intensity[1], intensity[0])

        @pl.when(last & (core == 1))
        def _():
            seen_out[...] = measured_whole
            seen_copy().start()

        @pl.when(split_core)
        def _():
            seen_in[...] = measured_split

        ext[...] = jnp.zeros_like(ext)
        canvas[...] = jnp.zeros_like(canvas)

        def gather_window(k):
            @pl.when(k // slab != core)
            def _():
                copy(
                    pair_out.at[k % slab], own_win.at[k], send_pair.at[k % slab],
                    recv_pair.at[k % slab], partner,
                ).wait_recv()

            @pl.when(split_core)
            def _():
                copy(
                    halo_out.at[k % slab], halo_win.at[k], send_halo.at[k % slab],
                    recv_halo.at[k], partner,
                ).wait_recv()
                ext[:, width:] = halo_win[k]

            ext[:, :width] = own_win[k]
            for part in range(2):
                win[k, part] = ext[part, pl.ds(rows, width), :]

        @pl.when(first)
        def _():
            waves[0] = probe[...]

        @pl.when(jnp.logical_not(first))
        def _():
            lax.fori_loop(0, count, lambda k, c: (gather_window(k), c)[1], 0)
            wave_copy().wait_recv()

        def forward(k, carry):
            @pl.when(first)
            def _():
                gather_window(k)

            real, imag = waves[k, 0], waves[k, 1]
            obj_real, obj_imag = win[k, 0], win[k, 1]
            real, imag = both_sides(
                real * obj_real - imag * obj_imag, real * obj_imag + imag * obj_real,
                right, left_high, left_low,
            )
            waves[k + 1, 0] = real
            waves[k + 1, 1] = imag
            return carry

        lax.fori_loop(0, count, forward, 0)

        @pl.when(jnp.logical_not(last))
        def _():
            wave_copy().start()
            copy(back, back_in, send_back, recv_back, partner).wait_recv()
            back[...] = back_in[...]

        @pl.when(last)
        def _():
            @pl.when(core == 1)
            def _():
                seen_copy().wait_recv()

            real, imag = both_sides(
                waves[count, 0], waves[count, 1], dft_right, dft_left_high, dft_left_low
            )
            misfit = 2.0 * (real * real + imag * imag - seen_in[...])
            real, imag = both_sides(
                misfit * real, -(misfit * imag), dft_right, dft_left_high, dft_left_low
            )
            back[0] = real
            back[1] = imag

        def hand_out(k):
            canvas[:, width:2 * width] = steps[k]
            own = [canvas[part, pl.ds(width - rows, width), :] for part in range(2)]
            at = k % slab

            @pl.when(k // slab == core)
            def _():
                for part in range(2):
                    mine[at, part] = own[part]

            @pl.when(k // slab != core)
            def _():
                for part in range(2):
                    pair_send[at, part] = own[part]
                grad_copy(at).start()

            @pl.when(split_core)
            def _():
                for part in range(2):
                    spill_out[k, part] = canvas[part, pl.ds(2 * width - rows, width), :]
                spill_copy(k).start()

        def backward(step, carry):
            k = count - 1 - step
            real, imag = both_sides(back[0], back[1], right, left_high, left_low)
            wave_real, wave_imag = waves[k, 0], waves[k, 1]
            obj_real, obj_imag = win[k, 0], win[k, 1]
            back[0] = obj_real * real - obj_imag * imag
            back[1] = obj_real * imag + obj_imag * real
            steps[k, 0] = wave_real * real - wave_imag * imag
            steps[k, 1] = -(wave_real * imag + wave_imag * real)

            @pl.when(first)
            def _():
                hand_out(k)

            return carry

        lax.fori_loop(0, count, backward, 0)

        @pl.when(jnp.logical_not(first))
        def _():
            back_copy().start()
            lax.fori_loop(0, count, lambda s, c: (hand_out(count - 1 - s), c)[1], 0)

        share = width // depth_count

        @pl.when(first)
        def _():
            for k in range(depth_count):
                chunks[k, 0] = back[0, k * share:(k + 1) * share]
                chunks[k, 1] = -back[1, k * share:(k + 1) * share]
            for k in range(1, depth_count):
                chunk_copy(k).start()
            parts[core] = chunks[dep]
            copy(chunks.at[0], parts.at[1 - core], send_chunk.at[0], recv_chunk.at[1 - core], partner).wait_recv()

        @pl.when(jnp.logical_not(first))
        def _():
            for k in range(2):
                copy(chunks.at[0], parts.at[k], send_chunk.at[0], recv_chunk.at[k], partner).wait_recv()

        value = parts[0] + parts[1]
        base = 0
        for level, clique in enumerate(cliques):
            total[level] = value
            hops = [
                copy(
                    total.at[level], around.at[base + k], send_around.at[base + k],
                    recv_around.at[base + k], device,
                )
                for k, device in enumerate(clique)
            ]
            for hop in hops:
                hop.start()
            for k, hop in enumerate(hops):
                hop.wait_recv()
                value = value + around[base + k]
            base += len(clique)
        probe_grad[...] = value

        blank = jnp.zeros((width, width), F32)

        def shifted_right(plane, amount):
            return pltpu.roll(jnp.concatenate([plane, blank], 1), amount, 1)

        for k in reversed(range(slab)):
            grad_copy(k).wait_recv()
            copy(spill_out.at[k], spill_in.at[k], send_spill.at[k], recv_spill.at[k], partner).wait_recv()
            for part in range(2):
                grad[k, part] = (
                    shifted_right(mine[k, part], col_mine)
                    + shifted_right(pair_in[k, part], col_pair)
                    + shifted_right(spill_in[k, part], col_before)
                )

        for k in range(slab):
            halo_copy(k).wait_send()
            pair_copy(k).wait_send()
            grad_copy(k).wait_send()

        @pl.when(last & (core == 1))
        def _():
            seen_copy().wait_send()

        @pl.when(split_core)
        def _():
            for k in range(count):
                spill_copy(k).wait_send()

        @pl.when(jnp.logical_not(last))
        def _():
            wave_copy().wait_send()

        @pl.when(jnp.logical_not(first))
        def _():
            back_copy().wait_send()

        @pl.when(first)
        def _():
            for k in range(1, depth_count):
                chunk_copy(k).wait_send()

        base = 0
        for level, clique in enumerate(cliques):
            for k, device in enumerate(clique):
                copy(
                    total.at[level], around.at[base + k], send_around.at[base + k],
                    recv_around.at[base + k], device,
                ).wait_send()
            base += len(clique)

    links = sum(side - 1 for side in sides)
    share = width // depth_count
    plane = (2, width, width)
    buffers = [
        (slab,) + plane, (slab,) + plane, (count,) + plane, (count,) + plane, (2, 2 * width, width),
        (count,) + plane, (count + 1,) + plane, plane, plane, (count,) + plane, (2, 3 * width, width),
        (slab,) + plane, (slab,) + plane, (slab,) + plane, (count,) + plane, (slab,) + plane,
        (width, width), (width, width), (depth_count, 2, share, width), (2, 2, share, width),
        (len(sides), 2, share, width), (links, 2, share, width),
    ]
    dma = pltpu.SemaphoreType.DMA
    marks = [
        dma((slab,)), dma((slab,)), dma, dma, dma((slab,)), dma((count,)), dma, dma((depth_count,)), dma((links,)),
        dma((count,)), dma((slab,)), dma, dma, dma((slab,)), dma((slab,)), dma, dma((2,)), dma((links,)),
    ]
    return kernel, [pltpu.VMEM(shape, F32) for shape in buffers] + marks


def body(objects, probe, row_offsets, col_offsets, intensity):
    slab, _, tile_rows, columns = objects.shape
    width = probe.shape[-1]
    depth_count = lax.axis_size("depth")
    scan_count = lax.axis_size("scan")
    me = lax.axis_index("scan")
    local_rows = row_offsets - me * tile_rows
    second = (local_rows[0] != tile_rows).astype(jnp.int32)
    col_whole = jnp.where(second == 1, col_offsets[1], col_offsets[0])
    col_split = jnp.where(second == 1, col_offsets[0], col_offsets[1])
    row_split = jnp.where(second == 1, local_rows[0], local_rows[1])
    route = [(k, (k + 1) % scan_count) for k in range(scan_count)]
    arrived = lax.ppermute(jnp.stack([col_whole, col_split]), "scan", route)
    zero = jnp.zeros((), jnp.int32)
    scalars = jnp.stack([col_split, row_split, arrived[0], arrived[1], second, zero, zero, zero])
    kernel, scratch = make_kernel(depth_count, scan_count, slab, width)
    tables = [jnp.asarray(table) for table in transfer_tables(width)]
    vmem = pl.BlockSpec(memory_space=pltpu.VMEM)
    return pl.pallas_call(
        kernel,
        out_shape=(
            jax.ShapeDtypeStruct(objects.shape, F32),
            jax.ShapeDtypeStruct((2, width // depth_count, width), F32),
        ),
        in_specs=[pl.BlockSpec(memory_space=pltpu.SMEM)] + [vmem] * 9,
        out_specs=(vmem, vmem),
        scratch_shapes=scratch,
        compiler_params=pltpu.CompilerParams(
            collective_id=0, has_side_effects=True, vmem_limit_bytes=48 << 20
        ),
        name="slices",
    )(scalars, objects, probe, intensity, *tables)


def solution(mesh):
    in_specs = (P("depth", None, "scan", None), P(), P("scan"), P("scan"), P("scan", None, None))
    out_specs = (P("depth", None, "scan", None), P(None, "depth", None))
    return jax.shard_map(body, mesh=mesh, in_specs=in_specs, out_specs=out_specs, check_vma=False)
```

```python
import jax
import jax.numpy as jnp
import ml_dtypes
import numpy as np
from jax import lax
from jax.experimental import pallas as pl
from jax.experimental.pallas import tpu as pltpu
from jax.sharding import PartitionSpec as P

PROPAGATION = 0.5
F32 = jnp.float32
BF16 = jnp.bfloat16
MESH = pl.DeviceIdType.MESH


def split_table(table):
    high = table.astype(ml_dtypes.bfloat16)
    low = (table - high.astype(np.float64)).astype(ml_dtypes.bfloat16)
    return high, low


def block_tables(matrix):
    real, imag = matrix.real, matrix.imag
    right_high, right_low = split_table(np.block([[real, imag], [-imag, real]]))
    left_high, left_low = split_table(np.block([[real, -imag], [imag, real]]))
    return np.concatenate([right_high, right_high, right_low], 0), left_high, left_low


def transfer_tables(width):
    index = np.arange(width)
    frequency = np.where(index < width // 2, index, index - width).astype(np.float64)
    fourier = np.exp(-2j * np.pi * (np.outer(index, index) % width) / width) / np.sqrt(width)
    chirp = np.exp(-1j * PROPAGATION * np.pi * frequency**2 / width)
    spread = fourier.conj() @ (chirp[:, None] * fourier)
    return block_tables(spread) + block_tables(fourier)


def grid_of(count):
    sides = []
    while count > 1:
        side = 4 if count % 4 == 0 else 2 if count % 2 == 0 else count
        sides.insert(0, side)
        count //= side
    return sides


def split(x):
    high = x.astype(BF16)
    return high, (x - high.astype(F32)).astype(BF16)


def dot(a, b):
    return jnp.dot(a, b, preferred_element_type=F32)


def both_sides(real, imag, right, left_high, left_low):
    width = real.shape[0]
    high, low = split(jnp.concatenate([real, imag], 1))
    mid = dot(jnp.concatenate([high, low, high], 1), right[...])
    high, low = split(jnp.concatenate([mid[:, :width], mid[:, width:]], 0))
    pair = dot(left_high[...], jnp.concatenate([high, low], 1))
    out = pair[:, :width] + pair[:, width:] + dot(left_low[...], high)
    return out[:width], out[width:]


def make_kernel(depth_count, scan_count, slab, width):
    stages = depth_count // 2
    count = 2 * slab
    sides = grid_of(scan_count)

    def kernel(
        row_hbm, col_hbm, objects_hbm, probe_hbm, intensity_hbm, *rest
    ):
        tables_hbm, rest = rest[:6], rest[6:]
        grad_hbm, probe_grad, *scratch = rest
        run(row_hbm, col_hbm, objects_hbm, probe_hbm, intensity_hbm, tables_hbm, grad_hbm, probe_grad, *scratch)

    def run(
        row_hbm, col_hbm, objects_hbm, probe_hbm, intensity_hbm, tables_hbm, grad_hbm, probe_grad,
        right, left_high, left_low, dft_right, dft_left_high, dft_left_low,
        objects, probe, intensity, grad, row_off, col_off, note_out, note_in,
        load_tables, load_objects, load_small, store_grad, send_note, recv_note,
        halo_out, pair_out, own_win, halo_win, ext, win, waves, back_in, back, steps, canvas,
        mine, pair_send, pair_in, spill_out, spill_in, seen_out, seen_in, chunks, parts, total, around,
        send_halo, send_pair, send_wave, send_back, send_grad, send_spill, send_seen, send_chunk, send_around,
        recv_halo, recv_pair, recv_wave, recv_back, recv_grad, recv_spill, recv_seen, recv_chunk, recv_around,
    ):
        dep = lax.axis_index("depth")
        me = lax.axis_index("scan")
        stage = dep // 2
        core = dep % 2
        first = stage == 0
        last = stage == stages - 1
        split_core = core == 0
        after = lax.rem(me + 1, scan_count)
        before = lax.rem(me + scan_count - 1, scan_count)
        partner = (dep + 1 - 2 * core, me)
        crew = [((lax.rem(dep + k, depth_count)), me) for k in range(1, depth_count)]
        cliques = []
        stride = scan_count
        for side in sides:
            stride //= side
            place = (me // stride) % side
            cliques.append(
                [(dep, me + (lax.rem(place + k, side) - place) * stride) for k in range(1, side)]
            )
        friends = crew + [(2 * stage + k, near) for near in (after, before) for k in range(2)]
        for clique in cliques:
            friends = friends + clique

        def copy(source, target, send, recv, device):
            return pltpu.make_async_remote_copy(
                src_ref=source, dst_ref=target, send_sem=send, recv_sem=recv,
                device_id=device, device_id_type=MESH,
            )

        def local(source, target, sem):
            return pltpu.make_async_copy(source, target, sem)

        barrier = pltpu.get_barrier_semaphore()
        for friend in friends:
            pl.semaphore_signal(barrier, inc=1, device_id=friend, device_id_type=MESH)

        loads = [local(row_hbm, row_off, load_small.at[0]), local(col_hbm, col_off, load_small.at[1])]
        object_loads = [local(objects_hbm.at[k], objects.at[k], load_objects.at[k]) for k in range(slab)]
        small_loads = [local(probe_hbm, probe, load_small.at[2]), local(intensity_hbm, intensity, load_small.at[3])]
        tables = [right, left_high, left_low, dft_right, dft_left_high, dft_left_low]
        table_loads = [local(tables_hbm[k], tables[k], load_tables.at[k]) for k in range(6)]
        for load in loads + object_loads + small_loads + table_loads:
            load.start()

        for load in loads:
            load.wait()
        rows_here = [row_off[k] - me * width for k in range(2)]
        second = rows_here[0] != width
        col_split = jnp.where(second, col_off[0], col_off[1])
        col_whole_here = jnp.where(second, col_off[1], col_off[0])
        row_split = jnp.where(second, rows_here[0], rows_here[1])
        rows = jnp.where(split_core, jnp.clip(row_split, 0, width), 0)
        note_out[0] = col_whole_here
        note_out[1] = col_split

        def note_copy():
            return copy(note_out, note_in, send_note, recv_note, (dep, after))

        def halo_copy(k):
            return copy(
                halo_out.at[k], halo_win.at[slab * core + k], send_halo.at[k],
                recv_halo.at[slab * core + k], (2 * stage, before),
            )

        def pair_copy(k):
            return copy(
                pair_out.at[k], own_win.at[slab * core + k], send_pair.at[k], recv_pair.at[k], partner
            )

        def seen_copy():
            return copy(seen_out, seen_in, send_seen, recv_seen, (dep, after))

        def wave_copy():
            return copy(waves.at[count], waves.at[0], send_wave, recv_wave, (dep + 2, me))

        def back_copy():
            return copy(back, back_in, send_back, recv_back, (dep - 2, me))

        def grad_copy(k):
            return copy(pair_send.at[k], pair_in.at[k], send_grad.at[k], recv_grad.at[k], partner)

        def spill_copy(k):
            return copy(
                spill_out.at[k], spill_in.at[k % slab], send_spill.at[k], recv_spill.at[k % slab],
                (2 * stage + k // slab, after),
            )

        def chunk_copy(k):
            target = lax.rem(dep + k, depth_count)
            return copy(
                chunks.at[target], parts.at[core], send_chunk.at[k], recv_chunk.at[core], (target, me)
            )

        def shifted_left(plane, amount):
            return pltpu.roll(plane, lax.rem(2 * width - amount, 2 * width), 1)[:, :width]

        for k in range(slab):
            object_loads[k].wait()
            for part in range(2):
                window = shifted_left(objects[k, part], col_split)

                @pl.when(split_core)
                def _():
                    own_win[k, part] = window

                @pl.when(jnp.logical_not(split_core))
                def _():
                    pair_out[k, part] = window

        pl.semaphore_wait(barrier, len(friends))
        note_copy().start()

        @pl.when(jnp.logical_not(split_core))
        def _():
            for k in range(slab):
                pair_copy(k).start()

        ext[...] = jnp.zeros_like(ext)
        canvas[...] = jnp.zeros_like(canvas)
        note_copy().wait_recv()
        col_whole = note_in[0]
        col_before = note_in[1]
        col_mine = jnp.where(split_core, col_split, col_whole)
        col_pair = jnp.where(split_core, col_whole, col_split)

        for k in range(slab):
            for part in range(2):
                halo_out[k, part] = shifted_left(objects[k, part], col_before)
            halo_copy(k).start()
            for part in range(2):
                window = shifted_left(objects[k, part], col_whole)

                @pl.when(split_core)
                def _():
                    pair_out[k, part] = window

                @pl.when(jnp.logical_not(split_core))
                def _():
                    own_win[slab + k, part] = window

            @pl.when(split_core)
            def _():
                pair_copy(k).start()

        for load in small_loads + table_loads:
            load.wait()
        measured_split = jnp.where(second, intensity[0], intensity[1])
        measured_whole = jnp.where(second, intensity[1], intensity[0])

        @pl.when(last & (core == 1))
        def _():
            seen_out[...] = measured_whole
            seen_copy().start()

        @pl.when(split_core)
        def _():
            seen_in[...] = measured_split

        def gather_window(k):
            @pl.when(k // slab != core)
            def _():
                copy(
                    pair_out.at[k % slab], own_win.at[k], send_pair.at[k % slab],
                    recv_pair.at[k % slab], partner,
                ).wait_recv()

            @pl.when(split_core)
            def _():
                copy(
                    halo_out.at[k % slab], halo_win.at[k], send_halo.at[k % slab],
                    recv_halo.at[k], partner,
                ).wait_recv()
                ext[:, width:] = halo_win[k]

            ext[:, :width] = own_win[k]
            for part in range(2):
                win[k, part] = ext[part, pl.ds(rows, width), :]

        @pl.when(first)
        def _():
            waves[0] = probe[...]

        @pl.when(jnp.logical_not(first))
        def _():
            lax.fori_loop(0, count, lambda k, c: (gather_window(k), c)[1], 0)
            wave_copy().wait_recv()

        def forward(k, carry):
            @pl.when(first)
            def _():
                gather_window(k)

            real, imag = waves[k, 0], waves[k, 1]
            obj_real, obj_imag = win[k, 0], win[k, 1]
            real, imag = both_sides(
                real * obj_real - imag * obj_imag, real * obj_imag + imag * obj_real,
                right, left_high, left_low,
            )
            waves[k + 1, 0] = real
            waves[k + 1, 1] = imag
            return carry

        lax.fori_loop(0, count, forward, 0)

        @pl.when(jnp.logical_not(last))
        def _():
            wave_copy().start()
            copy(back, back_in, send_back, recv_back, partner).wait_recv()
            back[...] = back_in[...]

        @pl.when(last)
        def _():
            @pl.when(core == 1)
            def _():
                seen_copy().wait_recv()

            real, imag = both_sides(
                waves[count, 0], waves[count, 1], dft_right, dft_left_high, dft_left_low
            )
            misfit = 2.0 * (real * real + imag * imag - seen_in[...])
            real, imag = both_sides(
                misfit * real, -(misfit * imag), dft_right, dft_left_high, dft_left_low
            )
            back[0] = real
            back[1] = imag

        def hand_out(k):
            canvas[:, width:2 * width] = steps[k]
            own = [canvas[part, pl.ds(width - rows, width), :] for part in range(2)]
            at = k % slab

            @pl.when(k // slab == core)
            def _():
                for part in range(2):
                    mine[at, part] = own[part]

            @pl.when(k // slab != core)
            def _():
                for part in range(2):
                    pair_send[at, part] = own[part]
                grad_copy(at).start()

            @pl.when(split_core)
            def _():
                for part in range(2):
                    spill_out[k, part] = canvas[part, pl.ds(2 * width - rows, width), :]
                spill_copy(k).start()

        def backward(step, carry):
            k = count - 1 - step
            real, imag = both_sides(back[0], back[1], right, left_high, left_low)
            wave_real, wave_imag = waves[k, 0], waves[k, 1]
            obj_real, obj_imag = win[k, 0], win[k, 1]
            back[0] = obj_real * real - obj_imag * imag
            back[1] = obj_real * imag + obj_imag * real
            steps[k, 0] = wave_real * real - wave_imag * imag
            steps[k, 1] = -(wave_real * imag + wave_imag * real)

            @pl.when(first & (step < 2))
            def _():
                hand_out(k)

            return carry

        lax.fori_loop(0, count, backward, 0)

        @pl.when(jnp.logical_not(first))
        def _():
            back_copy().start()

        share = width // depth_count

        @pl.when(first)
        def _():
            for k in range(depth_count):
                chunks[k, 0] = back[0, k * share:(k + 1) * share]
                chunks[k, 1] = -back[1, k * share:(k + 1) * share]
            for k in range(1, depth_count):
                chunk_copy(k).start()
            parts[core] = chunks[dep]

        lax.fori_loop(
            jnp.where(first, 2, 0), count, lambda s, c: (hand_out(count - 1 - s), c)[1], 0
        )

        @pl.when(first)
        def _():
            copy(chunks.at[0], parts.at[1 - core], send_chunk.at[0], recv_chunk.at[1 - core], partner).wait_recv()

        @pl.when(jnp.logical_not(first))
        def _():
            for k in range(2):
                copy(chunks.at[0], parts.at[k], send_chunk.at[0], recv_chunk.at[k], partner).wait_recv()

        value = parts[0] + parts[1]
        base = 0
        for level, clique in enumerate(cliques):
            total[level] = value
            hops = [
                copy(
                    total.at[level], around.at[base + k], send_around.at[base + k],
                    recv_around.at[base + k], device,
                )
                for k, device in enumerate(clique)
            ]
            for hop in hops:
                hop.start()
            for k, hop in enumerate(hops):
                hop.wait_recv()
                value = value + around[base + k]
            base += len(clique)
        probe_grad[...] = value

        blank = jnp.zeros((width, width), F32)

        def shifted_right(plane, amount):
            return pltpu.roll(jnp.concatenate([plane, blank], 1), amount, 1)

        for k in reversed(range(slab)):
            grad_copy(k).wait_recv()
            copy(spill_out.at[k], spill_in.at[k], send_spill.at[k], recv_spill.at[k], partner).wait_recv()
            for part in range(2):
                grad[k, part] = (
                    shifted_right(mine[k, part], col_mine)
                    + shifted_right(pair_in[k, part], col_pair)
                    + shifted_right(spill_in[k, part], col_before)
                )
            local(grad.at[k], grad_hbm.at[k], store_grad.at[k]).start()

        note_copy().wait_send()
        for k in range(slab):
            local(grad.at[k], grad_hbm.at[k], store_grad.at[k]).wait()
            halo_copy(k).wait_send()
            pair_copy(k).wait_send()
            grad_copy(k).wait_send()

        @pl.when(last & (core == 1))
        def _():
            seen_copy().wait_send()

        @pl.when(split_core)
        def _():
            for k in range(count):
                spill_copy(k).wait_send()

        @pl.when(jnp.logical_not(last))
        def _():
            wave_copy().wait_send()

        @pl.when(jnp.logical_not(first))
        def _():
            back_copy().wait_send()

        @pl.when(first)
        def _():
            for k in range(1, depth_count):
                chunk_copy(k).wait_send()

        base = 0
        for level, clique in enumerate(cliques):
            for k, device in enumerate(clique):
                copy(
                    total.at[level], around.at[base + k], send_around.at[base + k],
                    recv_around.at[base + k], device,
                ).wait_send()
            base += len(clique)

    links = sum(side - 1 for side in sides)
    share = width // depth_count
    plane = (2, width, width)
    buffers = [
        (slab,) + plane, (slab,) + plane, (count,) + plane, (count,) + plane, (2, 2 * width, width),
        (count,) + plane, (count + 1,) + plane, plane, plane, (count,) + plane, (2, 3 * width, width),
        (slab,) + plane, (slab,) + plane, (slab,) + plane, (count,) + plane, (slab,) + plane,
        (width, width), (width, width), (depth_count, 2, share, width), (2, 2, share, width),
        (len(sides), 2, share, width), (links, 2, share, width),
    ]
    dma = pltpu.SemaphoreType.DMA
    marks = [
        dma((slab,)), dma((slab,)), dma, dma, dma((slab,)), dma((count,)), dma, dma((depth_count,)), dma((links,)),
        dma((count,)), dma((slab,)), dma, dma, dma((slab,)), dma((slab,)), dma, dma((2,)), dma((links,)),
    ]
    square = (2 * width, 2 * width)
    tables = [(6 * width, 2 * width), square, square] * 2
    inputs = [(slab, 2, width, 2 * width), plane, plane, (slab, 2, width, 2 * width)]
    head = [pltpu.VMEM(shape, BF16) for shape in tables] + [pltpu.VMEM(shape, F32) for shape in inputs]
    head += [pltpu.SMEM((2,), jnp.int32)] * 4
    head += [dma((6,)), dma((slab,)), dma((4,)), dma((slab,)), dma, dma]
    return kernel, head + [pltpu.VMEM(shape, F32) for shape in buffers] + marks


def body(objects, probe, row_offsets, col_offsets, intensity):
    slab = objects.shape[0]
    width = probe.shape[-1]
    depth_count = lax.axis_size("depth")
    scan_count = lax.axis_size("scan")
    kernel, scratch = make_kernel(depth_count, scan_count, slab, width)
    tables = [jnp.asarray(table) for table in transfer_tables(width)]
    vmem = pl.BlockSpec(memory_space=pltpu.VMEM)
    anywhere = pl.BlockSpec(memory_space=pl.ANY)
    return pl.pallas_call(
        kernel,
        out_shape=(
            jax.ShapeDtypeStruct(objects.shape, F32),
            jax.ShapeDtypeStruct((2, width // depth_count, width), F32),
        ),
        in_specs=[anywhere] * 11,
        out_specs=(anywhere, vmem),
        scratch_shapes=scratch,
        compiler_params=pltpu.CompilerParams(
            collective_id=0, has_side_effects=True, vmem_limit_bytes=56 << 20
        ),
        name="slices",
    )(row_offsets, col_offsets, objects, probe, intensity, *tables)


def solution(mesh):
    in_specs = (P("depth", None, "scan", None), P(), P("scan"), P("scan"), P("scan", None, None))
    out_specs = (P("depth", None, "scan", None), P(None, "depth", None))
    return jax.shard_map(body, mesh=mesh, in_specs=in_specs, out_specs=out_specs, check_vma=False)
```

```python
import jax
import jax.numpy as jnp
import ml_dtypes
import numpy as np
from jax import lax
from jax.experimental import pallas as pl
from jax.experimental.pallas import tpu as pltpu
from jax.sharding import PartitionSpec as P

PROPAGATION = 0.5
F32 = jnp.float32
BF16 = jnp.bfloat16
MESH = pl.DeviceIdType.MESH


def split_table(table):
    high = table.astype(ml_dtypes.bfloat16)
    low = (table - high.astype(np.float64)).astype(ml_dtypes.bfloat16)
    return high, low


def block_tables(matrix):
    real, imag = matrix.real, matrix.imag
    right_high, right_low = split_table(np.block([[real, imag], [-imag, real]]))
    left_high, left_low = split_table(np.block([[real, -imag], [imag, real]]))
    return np.concatenate([right_high, right_high, right_low], 0), left_high, left_low


def transfer_tables(width):
    index = np.arange(width)
    frequency = np.where(index < width // 2, index, index - width).astype(np.float64)
    fourier = np.exp(-2j * np.pi * (np.outer(index, index) % width) / width) / np.sqrt(width)
    chirp = np.exp(-1j * PROPAGATION * np.pi * frequency**2 / width)
    spread = fourier.conj() @ (chirp[:, None] * fourier)
    return block_tables(spread) + block_tables(fourier)


def groups_of(count):
    return [16, count // 16] if count % 16 == 0 and count > 16 else [count]


def split(x):
    high = x.astype(BF16)
    return high, (x - high.astype(F32)).astype(BF16)


def dot(a, b):
    return jnp.dot(a, b, preferred_element_type=F32)


def both_sides(real, imag, right, left_high, left_low):
    width = real.shape[0]
    high, low = split(jnp.concatenate([real, imag], 1))
    mid = dot(jnp.concatenate([high, low, high], 1), right[...])
    high, low = split(jnp.concatenate([mid[:, :width], mid[:, width:]], 0))
    pair = dot(left_high[...], jnp.concatenate([high, low], 1))
    out = pair[:, :width] + pair[:, width:] + dot(left_low[...], high)
    return out[:width], out[width:]


def make_kernel(depth_count, scan_count, slab, width):
    stages = depth_count // 2
    count = 2 * slab
    sides = groups_of(scan_count)
    early = min(2, slab)

    def kernel(
        row_hbm, col_hbm, objects_hbm, probe_hbm, intensity_hbm, *rest
    ):
        tables_hbm, rest = rest[:6], rest[6:]
        grad, probe_grad, *scratch = rest
        run(row_hbm, col_hbm, objects_hbm, probe_hbm, intensity_hbm, tables_hbm, grad, probe_grad, *scratch)

    def run(
        row_hbm, col_hbm, objects_hbm, probe_hbm, intensity_hbm, tables_hbm, grad, probe_grad,
        right, left_high, left_low, dft_right, dft_left_high, dft_left_low,
        objects, probe, intensity, row_off, col_off, note_out, note_in,
        load_tables, load_objects, load_small, send_note, recv_note,
        early_win, far_parts, far_sum, recv_far, send_relay,
        halo_out, pair_out, own_win, halo_win, ext, win, waves, back_in, back, steps, canvas,
        mine, pair_send, pair_in, spill_out, spill_in, seen_out, seen_in, chunks, parts, total, around,
        send_halo, send_pair, send_wave, send_back, send_grad, send_spill, send_seen, send_chunk, send_around,
        recv_halo, recv_pair, recv_wave, recv_back, recv_grad, recv_spill, recv_seen, recv_chunk, recv_around,
    ):
        dep = lax.axis_index("depth")
        me = lax.axis_index("scan")
        stage = dep // 2
        core = dep % 2
        first = stage == 0
        last = stage == stages - 1
        split_core = core == 0
        after = lax.rem(me + 1, scan_count)
        before = lax.rem(me + scan_count - 1, scan_count)
        partner = (dep + 1 - 2 * core, me)
        ahead = lax.rem(stage + 1, stages)
        behind = lax.rem(stage + stages - 1, stages)
        crew = [partner] + [(2 * near + k, me) for near in (ahead, behind) for k in range(2)]
        cliques = []
        stride = 1
        for side in sides:
            place = (me // stride) % side
            cliques.append(
                [(dep, me + (lax.rem(place + k, side) - place) * stride) for k in range(1, side)]
            )
            stride *= side
        friends = crew + [(2 * stage + k, near) for near in (after, before) for k in range(2)]
        for clique in cliques:
            friends = friends + clique

        def copy(source, target, send, recv, device):
            return pltpu.make_async_remote_copy(
                src_ref=source, dst_ref=target, send_sem=send, recv_sem=recv,
                device_id=device, device_id_type=MESH,
            )

        def local(source, target, sem):
            return pltpu.make_async_copy(source, target, sem)

        barrier = pltpu.get_barrier_semaphore()
        for friend in friends:
            pl.semaphore_signal(barrier, inc=1, device_id=friend, device_id_type=MESH)

        loads = [local(row_hbm, row_off, load_small.at[0]), local(col_hbm, col_off, load_small.at[1])]
        object_loads = [local(objects_hbm.at[k], objects.at[k], load_objects.at[k]) for k in range(slab)]
        small_loads = [local(probe_hbm, probe, load_small.at[2]), local(intensity_hbm, intensity, load_small.at[3])]
        tables = [right, left_high, left_low, dft_right, dft_left_high, dft_left_low]
        table_loads = [local(tables_hbm[k], tables[k], load_tables.at[k]) for k in range(6)]
        for load in loads + object_loads + small_loads + table_loads:
            load.start()

        for load in loads:
            load.wait()
        rows_here = [row_off[k] - me * width for k in range(2)]
        second = rows_here[0] != width
        col_split = jnp.where(second, col_off[0], col_off[1])
        col_whole_here = jnp.where(second, col_off[1], col_off[0])
        row_split = jnp.where(second, rows_here[0], rows_here[1])
        rows = jnp.where(split_core, jnp.clip(row_split, 0, width), 0)
        note_out[0] = col_whole_here
        note_out[1] = col_split

        def note_copy():
            return copy(note_out, note_in, send_note, recv_note, (dep, after))

        def halo_copy(k):
            return copy(
                halo_out.at[k], halo_win.at[slab * core + k], send_halo.at[k],
                recv_halo.at[slab * core + k], (2 * stage, before),
            )

        def early_copy(k):
            return copy(
                objects.at[k], early_win.at[k], send_halo.at[k], recv_halo.at[k], (2 * stage, before)
            )

        def pair_copy(k):
            return copy(
                pair_out.at[k], own_win.at[slab * core + k], send_pair.at[k], recv_pair.at[k], partner
            )

        def seen_copy():
            return copy(seen_out, seen_in, send_seen, recv_seen, (dep, after))

        def wave_copy():
            return copy(waves.at[count], waves.at[0], send_wave, recv_wave, (dep + 2, me))

        def back_copy():
            return copy(back, back_in, send_back, recv_back, (dep - 2, me))

        def grad_copy(k):
            return copy(pair_send.at[k], pair_in.at[k], send_grad.at[k], recv_grad.at[k], partner)

        def spill_copy(k):
            return copy(
                spill_out.at[k], spill_in.at[k % slab], send_spill.at[k], recv_spill.at[k % slab],
                (2 * stage + k // slab, after),
            )

        def chunk_copy(target, core_from):
            if target // 2 == 2 and stages == 4:
                way = 2 if target % 2 == 0 else 7
                return copy(
                    chunks.at[target], far_parts.at[core_from], send_chunk.at[target], recv_far.at[core_from], (way, me)
                )
            return copy(
                chunks.at[target], parts.at[core_from], send_chunk.at[target], recv_chunk.at[core_from], (target, me)
            )

        def relay_copy():
            target = jnp.where(dep == 2, 4, 5)
            return copy(far_sum, parts.at[0], send_relay, recv_chunk.at[0], (target, me))

        def shifted_left(plane, amount):
            return pltpu.roll(plane, lax.rem(2 * width - amount, 2 * width), 1)[:, :width]

        for k in range(slab):
            object_loads[k].wait()
            for part in range(2):
                window = shifted_left(objects[k, part], col_split)

                @pl.when(split_core)
                def _():
                    own_win[k, part] = window

                @pl.when(jnp.logical_not(split_core))
                def _():
                    pair_out[k, part] = window

        pl.semaphore_wait(barrier, len(friends))
        note_copy().start()

        @pl.when(split_core)
        def _():
            for k in range(early):
                early_copy(k).start()

        @pl.when(jnp.logical_not(split_core))
        def _():
            for k in range(slab):
                pair_copy(k).start()

        ext[...] = jnp.zeros_like(ext)
        canvas[...] = jnp.zeros_like(canvas)
        note_copy().wait_recv()
        col_whole = note_in[0]
        col_before = note_in[1]
        col_mine = jnp.where(split_core, col_split, col_whole)
        col_pair = jnp.where(split_core, col_whole, col_split)

        for k in range(slab):
            for part in range(2):
                window = shifted_left(objects[k, part], col_whole)

                @pl.when(split_core)
                def _():
                    pair_out[k, part] = window

                @pl.when(jnp.logical_not(split_core))
                def _():
                    own_win[slab + k, part] = window

            @pl.when(split_core)
            def _():
                pair_copy(k).start()

        for k in range(slab):
            def send_window():
                for part in range(2):
                    halo_out[k, part] = shifted_left(objects[k, part], col_before)
                halo_copy(k).start()

            if k < early:
                pl.when(jnp.logical_not(split_core))(send_window)
            else:
                send_window()

        for load in small_loads + table_loads:
            load.wait()
        measured_split = jnp.where(second, intensity[0], intensity[1])
        measured_whole = jnp.where(second, intensity[1], intensity[0])

        @pl.when(last & (core == 1))
        def _():
            seen_out[...] = measured_whole
            seen_copy().start()

        @pl.when(split_core)
        def _():
            seen_in[...] = measured_split

        def gather_window(k):
            @pl.when(core != k // slab)
            def _():
                copy(
                    pair_out.at[k % slab], own_win.at[k], send_pair.at[k % slab],
                    recv_pair.at[k % slab], partner,
                ).wait_recv()

            @pl.when(split_core)
            def _():
                if k < early:
                    early_copy(k).wait_recv()
                    for part in range(2):
                        ext[part, width:] = shifted_left(early_win[k, part], col_split)
                else:
                    copy(
                        halo_out.at[k % slab], halo_win.at[k], send_halo.at[k % slab],
                        recv_halo.at[k], partner,
                    ).wait_recv()
                    ext[:, width:] = halo_win[k]

            ext[:, :width] = own_win[k]
            for part in range(2):
                win[k, part] = ext[part, pl.ds(rows, width), :]

        def forward(k, real, imag):
            obj_real, obj_imag = win[k, 0], win[k, 1]
            real, imag = both_sides(
                real * obj_real - imag * obj_imag, real * obj_imag + imag * obj_real,
                right, left_high, left_low,
            )
            waves[k + 1, 0] = real
            waves[k + 1, 1] = imag
            return real, imag

        @pl.when(first)
        def _():
            waves[0] = probe[...]
            for k in range(count):
                gather_window(k)
                forward(k, waves[k, 0], waves[k, 1])

        @pl.when(jnp.logical_not(first))
        def _():
            for k in range(count):
                gather_window(k)
            wave_copy().wait_recv()
            real, imag = waves[0, 0], waves[0, 1]
            for k in range(count):
                real, imag = forward(k, real, imag)

        @pl.when(jnp.logical_not(last))
        def _():
            wave_copy().start()
            copy(back, back_in, send_back, recv_back, partner).wait_recv()
            back[...] = back_in[...]

        @pl.when(last)
        def _():
            @pl.when(core == 1)
            def _():
                seen_copy().wait_recv()

            real, imag = both_sides(
                waves[count, 0], waves[count, 1], dft_right, dft_left_high, dft_left_low
            )
            misfit = 2.0 * (real * real + imag * imag - seen_in[...])
            real, imag = both_sides(
                misfit * real, -(misfit * imag), dft_right, dft_left_high, dft_left_low
            )
            back[0] = real
            back[1] = imag

        def hand_out(k):
            canvas[:, width:2 * width] = steps[k]
            own = [canvas[part, pl.ds(width - rows, width), :] for part in range(2)]
            at = k % slab

            @pl.when(k // slab == core)
            def _():
                for part in range(2):
                    mine[at, part] = own[part]

            @pl.when(k // slab != core)
            def _():
                for part in range(2):
                    pair_send[at, part] = own[part]
                grad_copy(at).start()

            @pl.when(split_core)
            def _():
                for part in range(2):
                    spill_out[k, part] = canvas[part, pl.ds(2 * width - rows, width), :]
                spill_copy(k).start()

        real, imag = back[0], back[1]
        for k in reversed(range(count)):
            real, imag = both_sides(real, imag, right, left_high, left_low)
            wave_real, wave_imag = waves[k, 0], waves[k, 1]
            obj_real, obj_imag = win[k, 0], win[k, 1]
            steps[k, 0] = wave_real * real - wave_imag * imag
            steps[k, 1] = -(wave_real * imag + wave_imag * real)
            real, imag = obj_real * real - obj_imag * imag, obj_real * imag + obj_imag * real
        back[0] = real
        back[1] = imag

        @pl.when(jnp.logical_not(first))
        def _():
            back_copy().start()

        share = width // depth_count

        @pl.when(first)
        def _():
            for k in range(depth_count):
                chunks[k, 0] = back[0, k * share:(k + 1) * share]
                chunks[k, 1] = -back[1, k * share:(k + 1) * share]
            for side in range(2):
                @pl.when(core == side)
                def _():
                    for k in range(depth_count):
                        if k != side:
                            chunk_copy(k, side).start()
                    parts[side] = chunks[side]

        lax.fori_loop(0, count, lambda s, c: (hand_out(count - 1 - s), c)[1], 0)

        def await_chunk(k):
            copy(chunks.at[0], parts.at[k], send_chunk.at[0], recv_chunk.at[k], partner).wait_recv()

        if stages == 4:
            @pl.when((dep == 2) | (dep == 7))
            def _():
                for k in range(2):
                    copy(chunks.at[0], far_parts.at[k], send_chunk.at[0], recv_far.at[k], partner).wait_recv()
                far_sum[...] = far_parts[0] + far_parts[1]
                relay_copy().start()

        @pl.when(first)
        def _():
            await_chunk(1 - core)

        @pl.when((stage == 1) | (stage == 3))
        def _():
            await_chunk(0)
            await_chunk(1)

        @pl.when(stage == 2)
        def _():
            await_chunk(0)
            parts[1] = jnp.zeros_like(parts[1])

        blank = jnp.zeros((width, width), F32)

        def shifted_right(plane, amount):
            return pltpu.roll(jnp.concatenate([plane, blank], 1), amount, 1)

        def add_up(k):
            grad_copy(k).wait_recv()
            copy(spill_out.at[k], spill_in.at[k], send_spill.at[k], recv_spill.at[k], partner).wait_recv()
            for part in range(2):
                grad[k, part] = (
                    shifted_right(mine[k, part], col_mine)
                    + shifted_right(pair_in[k, part], col_pair)
                    + shifted_right(spill_in[k, part], col_before)
                )

        value = parts[0] + parts[1]
        base = 0
        for level, clique in enumerate(cliques):
            total[level] = value
            hops = [
                copy(
                    total.at[level], around.at[base + k], send_around.at[base + k],
                    recv_around.at[base + k], device,
                )
                for k, device in enumerate(clique)
            ]
            for hop in hops:
                hop.start()
            for k in range(slab):
                if (level == 0) == (k > 0) or len(cliques) == 1:
                    add_up(k)
            for k, hop in enumerate(hops):
                hop.wait_recv()
                value = value + around[base + k]
            base += len(clique)
        probe_grad[...] = value

        note_copy().wait_send()
        for k in range(slab):
            if k < early:
                pl.when(split_core)(lambda: early_copy(k).wait_send())
                pl.when(jnp.logical_not(split_core))(lambda: halo_copy(k).wait_send())
            else:
                halo_copy(k).wait_send()
            pair_copy(k).wait_send()
            grad_copy(k).wait_send()

        @pl.when(last & (core == 1))
        def _():
            seen_copy().wait_send()

        @pl.when(split_core)
        def _():
            for k in range(count):
                spill_copy(k).wait_send()

        @pl.when(jnp.logical_not(last))
        def _():
            wave_copy().wait_send()

        @pl.when(jnp.logical_not(first))
        def _():
            back_copy().wait_send()

        @pl.when(first)
        def _():
            for side in range(2):
                @pl.when(core == side)
                def _():
                    for k in range(depth_count):
                        if k != side:
                            chunk_copy(k, side).wait_send()

        if stages == 4:
            @pl.when((dep == 2) | (dep == 7))
            def _():
                relay_copy().wait_send()

        base = 0
        for level, clique in enumerate(cliques):
            for k, device in enumerate(clique):
                copy(
                    total.at[level], around.at[base + k], send_around.at[base + k],
                    recv_around.at[base + k], device,
                ).wait_send()
            base += len(clique)

    links = sum(side - 1 for side in sides)
    share = width // depth_count
    plane = (2, width, width)
    buffers = [
        (slab,) + plane, (slab,) + plane, (count,) + plane, (count,) + plane, (2, 2 * width, width),
        (count,) + plane, (count + 1,) + plane, plane, plane, (count,) + plane, (2, 3 * width, width),
        (slab,) + plane, (slab,) + plane, (slab,) + plane, (count,) + plane, (slab,) + plane,
        (width, width), (width, width), (depth_count, 2, share, width), (2, 2, share, width),
        (len(sides), 2, share, width), (links, 2, share, width),
    ]
    dma = pltpu.SemaphoreType.DMA
    marks = [
        dma((slab,)), dma((slab,)), dma, dma, dma((slab,)), dma((count,)), dma, dma((depth_count,)), dma((links,)),
        dma((count,)), dma((slab,)), dma, dma, dma((slab,)), dma((slab,)), dma, dma((2,)), dma((links,)),
    ]
    square = (2 * width, 2 * width)
    tables = [(6 * width, 2 * width), square, square] * 2
    inputs = [(slab, 2, width, 2 * width), plane, plane]
    head = [pltpu.VMEM(shape, BF16) for shape in tables] + [pltpu.VMEM(shape, F32) for shape in inputs]
    head += [pltpu.SMEM((2,), jnp.int32)] * 4
    head += [dma((6,)), dma((slab,)), dma((4,)), dma, dma]
    piece = (2, share, width)
    head += [pltpu.VMEM((early, 2, width, 2 * width), F32), pltpu.VMEM((2,) + piece, F32), pltpu.VMEM(piece, F32)]
    head += [dma((2,)), dma]
    return kernel, head + [pltpu.VMEM(shape, F32) for shape in buffers] + marks


def body(objects, probe, row_offsets, col_offsets, intensity):
    slab = objects.shape[0]
    width = probe.shape[-1]
    depth_count = lax.axis_size("depth")
    scan_count = lax.axis_size("scan")
    kernel, scratch = make_kernel(depth_count, scan_count, slab, width)
    tables = [jnp.asarray(table) for table in transfer_tables(width)]
    vmem = pl.BlockSpec(memory_space=pltpu.VMEM)
    anywhere = pl.BlockSpec(memory_space=pl.ANY)
    return pl.pallas_call(
        kernel,
        out_shape=(
            jax.ShapeDtypeStruct(objects.shape, F32),
            jax.ShapeDtypeStruct((2, width // depth_count, width), F32),
        ),
        in_specs=[anywhere] * 11,
        out_specs=(vmem, vmem),
        scratch_shapes=scratch,
        compiler_params=pltpu.CompilerParams(
            collective_id=0, has_side_effects=True, vmem_limit_bytes=56 << 20
        ),
        name="slices",
    )(row_offsets, col_offsets, objects, probe, intensity, *tables)


def solution(mesh):
    in_specs = (P("depth", None, "scan", None), P(), P("scan"), P("scan"), P("scan", None, None))
    out_specs = (P("depth", None, "scan", None), P(None, "depth", None))
    return jax.shard_map(body, mesh=mesh, in_specs=in_specs, out_specs=out_specs, check_vma=False)
```

```python
import jax
import jax.numpy as jnp
import ml_dtypes
import numpy as np
from jax import lax
from jax.experimental import pallas as pl
from jax.experimental.pallas import tpu as pltpu
from jax.sharding import PartitionSpec as P

PROPAGATION = 0.5
F32 = jnp.float32
BF16 = jnp.bfloat16
MESH = pl.DeviceIdType.MESH


def split_table(table):
    high = table.astype(ml_dtypes.bfloat16)
    low = (table - high.astype(np.float64)).astype(ml_dtypes.bfloat16)
    return high, low


def block_tables(matrix):
    real, imag = matrix.real, matrix.imag
    right_high, right_low = split_table(np.block([[real, imag], [-imag, real]]))
    left_high, left_low = split_table(np.block([[real, -imag], [imag, real]]))
    return np.concatenate([right_high, right_high, right_low], 0), left_high, left_low


def transfer_tables(width):
    index = np.arange(width)
    frequency = np.where(index < width // 2, index, index - width).astype(np.float64)
    fourier = np.exp(-2j * np.pi * (np.outer(index, index) % width) / width) / np.sqrt(width)
    chirp = np.exp(-1j * PROPAGATION * np.pi * frequency**2 / width)
    spread = fourier.conj() @ (chirp[:, None] * fourier)
    return block_tables(spread) + block_tables(fourier)


def groups_of(count):
    return [16, count // 16] if count % 16 == 0 and count > 16 else [count]


def split(x):
    high = x.astype(BF16)
    return high, (x - high.astype(F32)).astype(BF16)


def dot(a, b):
    return jnp.dot(a, b, preferred_element_type=F32)


def both_sides(real, imag, right, left_high, left_low):
    width = real.shape[0]
    high, low = split(jnp.concatenate([real, imag], 1))
    mid = dot(jnp.concatenate([high, low, high], 1), right[...])
    high, low = split(jnp.concatenate([mid[:, :width], mid[:, width:]], 0))
    pair = dot(left_high[...], jnp.concatenate([high, low], 1))
    out = pair[:, :width] + pair[:, width:] + dot(left_low[...], high)
    return out[:width], out[width:]


def make_kernel(depth_count, scan_count, slab, width):
    stages = depth_count // 2
    count = 2 * slab
    sides = groups_of(scan_count)
    early = slab

    def kernel(
        row_hbm, col_hbm, objects_hbm, probe_hbm, intensity_hbm, *rest
    ):
        tables_hbm, rest = rest[:6], rest[6:]
        run(row_hbm, col_hbm, objects_hbm, probe_hbm, intensity_hbm, tables_hbm, *rest)

    def run(
        row_hbm, col_hbm, objects_hbm, probe_hbm, intensity_hbm, tables_hbm, grad, spill_grad, probe_grad, probe_rest,
        right, left_high, left_low, dft_right, dft_left_high, dft_left_low,
        objects, probe, intensity, row_off, col_off, note_out, note_in,
        load_tables, load_objects, load_small, send_note, recv_note,
        early_win,
        halo_out, pair_out, own_win, halo_win, ext, win, waves, back_in, back, steps, canvas,
        mine, pair_send, pair_in, spill_out, spill_in, seen_out, seen_in, chunks, parts, total, around,
        send_halo, send_pair, send_wave, send_back, send_grad, send_spill, send_seen, send_chunk, send_around,
        recv_halo, recv_pair, recv_wave, recv_back, recv_grad, recv_spill, recv_seen, recv_chunk, recv_around,
    ):
        dep = lax.axis_index("depth")
        me = lax.axis_index("scan")
        stage = dep // 2
        core = dep % 2
        first = stage == 0
        last = stage == stages - 1
        split_core = core == 1
        after = lax.rem(me + 1, scan_count)
        before = lax.rem(me + scan_count - 1, scan_count)
        partner = (dep + 1 - 2 * core, me)
        ahead = lax.rem(stage + 1, stages)
        behind = lax.rem(stage + stages - 1, stages)
        crew = [partner] + [(2 * near + k, me) for near in (ahead, behind) for k in range(2)]
        cliques = []
        stride = 1
        for side in sides:
            place = (me // stride) % side
            cliques.append(
                [(dep, me + (lax.rem(place + k, side) - place) * stride) for k in range(1, side)]
            )
            stride *= side
        friends = crew + [(2 * stage + k, near) for near in (after, before) for k in range(2)]
        for clique in cliques:
            friends = friends + clique

        def copy(source, target, send, recv, device):
            return pltpu.make_async_remote_copy(
                src_ref=source, dst_ref=target, send_sem=send, recv_sem=recv,
                device_id=device, device_id_type=MESH,
            )

        def local(source, target, sem):
            return pltpu.make_async_copy(source, target, sem)

        barrier = pltpu.get_barrier_semaphore()
        for friend in friends:
            pl.semaphore_signal(barrier, inc=1, device_id=friend, device_id_type=MESH)

        loads = [local(row_hbm, row_off, load_small.at[0]), local(col_hbm, col_off, load_small.at[1])]
        object_loads = [local(objects_hbm.at[k], objects.at[k], load_objects.at[k]) for k in range(slab)]
        small_loads = [local(probe_hbm, probe, load_small.at[2]), local(intensity_hbm, intensity, load_small.at[3])]
        tables = [right, left_high, left_low, dft_right, dft_left_high, dft_left_low]
        table_loads = [local(tables_hbm[k], tables[k], load_tables.at[k]) for k in range(6)]
        for load in loads + object_loads + small_loads + table_loads:
            load.start()

        for load in loads:
            load.wait()
        rows_here = [row_off[k] - me * width for k in range(2)]
        second = rows_here[0] != width
        col_split = jnp.where(second, col_off[0], col_off[1])
        col_whole_here = jnp.where(second, col_off[1], col_off[0])
        row_split = jnp.where(second, rows_here[0], rows_here[1])
        rows = jnp.where(split_core, jnp.clip(row_split, 0, width), 0)
        note_out[0] = col_whole_here
        note_out[1] = col_split

        def note_copy():
            return copy(note_out, note_in, send_note, recv_note, (dep, after))

        def halo_copy(k):
            return copy(
                halo_out.at[k], halo_win.at[slab * core + k], send_halo.at[k],
                recv_halo.at[slab * core + k], (2 * stage + 1, before),
            )

        def early_copy(k):
            return copy(
                objects.at[k], early_win.at[k], send_halo.at[k], recv_halo.at[k], (2 * stage + 1, before)
            )

        def pair_copy(k):
            return copy(
                pair_out.at[k], own_win.at[slab * core + k], send_pair.at[k], recv_pair.at[k], partner
            )

        def seen_copy():
            return copy(seen_out, seen_in, send_seen, recv_seen, (dep, after))

        def wave_copy():
            return copy(waves.at[count], waves.at[0], send_wave, recv_wave, (dep + 2, me))

        def back_copy():
            return copy(back, back_in, send_back, recv_back, (dep - 2, me))

        def grad_copy(k):
            return copy(pair_send.at[k], pair_in.at[k], send_grad.at[k], recv_grad.at[k], partner)

        def spill_copy(k):
            return copy(
                spill_out.at[k], spill_in.at[k % slab], send_spill.at[k], recv_spill.at[k % slab],
                (2 * stage + k // slab, after),
            )

        def chunk_copy(target, core_from):
            return copy(
                chunks.at[target], parts.at[core_from], send_chunk.at[target], recv_chunk.at[core_from], (target, me)
            )

        def shifted_left(plane, amount):
            return pltpu.roll(plane, lax.rem(2 * width - amount, 2 * width), 1)[:, :width]

        for k in range(slab):
            object_loads[k].wait()
            for part in range(2):
                window = shifted_left(objects[k, part], col_split)

                @pl.when(split_core)
                def _():
                    own_win[slab + k, part] = window

                @pl.when(jnp.logical_not(split_core))
                def _():
                    pair_out[k, part] = window

        pl.semaphore_wait(barrier, len(friends))
        note_copy().start()

        @pl.when(core == 0)
        def _():
            for k in range(slab):
                pair_copy(k).start()
            for k in range(early):
                early_copy(k).start()

        ext[...] = jnp.zeros_like(ext)
        canvas[...] = jnp.zeros_like(canvas)
        note_copy().wait_recv()
        col_whole = note_in[0]
        col_before = note_in[1]
        col_mine = jnp.where(split_core, col_split, col_whole)
        col_pair = jnp.where(split_core, col_whole, col_split)

        for k in range(slab):
            for part in range(2):
                window = shifted_left(objects[k, part], col_whole)

                @pl.when(core == 0)
                def _():
                    own_win[k, part] = window

                @pl.when(core == 1)
                def _():
                    pair_out[k, part] = window

            @pl.when(core == 1)
            def _():
                pair_copy(k).start()

        @pl.when(core == 1)
        def _():
            for k in range(slab):
                for part in range(2):
                    halo_out[k, part] = shifted_left(objects[k, part], col_before)
                halo_copy(k).start()

        for load in small_loads + table_loads:
            load.wait()
        measured_split = jnp.where(second, intensity[0], intensity[1])
        measured_whole = jnp.where(second, intensity[1], intensity[0])

        @pl.when(last & (core == 0))
        def _():
            seen_out[...] = measured_whole
            seen_copy().start()

        @pl.when(split_core)
        def _():
            seen_in[...] = measured_split

        def gather_window(k):
            @pl.when(core != k // slab)
            def _():
                copy(
                    pair_out.at[k % slab], own_win.at[k], send_pair.at[k % slab],
                    recv_pair.at[k % slab], partner,
                ).wait_recv()

            @pl.when(split_core)
            def _():
                if k < early:
                    early_copy(k).wait_recv()
                    for part in range(2):
                        ext[part, width:] = shifted_left(early_win[k, part], col_split)
                else:
                    copy(
                        halo_out.at[k % slab], halo_win.at[k], send_halo.at[k % slab],
                        recv_halo.at[k], partner,
                    ).wait_recv()
                    ext[:, width:] = halo_win[k]

            ext[:, :width] = own_win[k]
            for part in range(2):
                win[k, part] = ext[part, pl.ds(rows, width), :]

        def forward(k, real, imag):
            obj_real, obj_imag = win[k, 0], win[k, 1]
            real, imag = both_sides(
                real * obj_real - imag * obj_imag, real * obj_imag + imag * obj_real,
                right, left_high, left_low,
            )
            waves[k + 1, 0] = real
            waves[k + 1, 1] = imag
            return real, imag

        @pl.when(first)
        def _():
            waves[0] = probe[...]
            for k in range(count):
                gather_window(k)
                forward(k, waves[k, 0], waves[k, 1])

        @pl.when(jnp.logical_not(first))
        def _():
            for k in range(count):
                gather_window(k)
            wave_copy().wait_recv()
            real, imag = waves[0, 0], waves[0, 1]
            for k in range(count - 1):
                real, imag = forward(k, real, imag)

            @pl.when(jnp.logical_not(last))
            def _():
                forward(count - 1, real, imag)

        def step_back(k, real, imag):
            wave_real, wave_imag = waves[k, 0], waves[k, 1]
            obj_real, obj_imag = win[k, 0], win[k, 1]
            steps[k, 0] = wave_real * real - wave_imag * imag
            steps[k, 1] = -(wave_real * imag + wave_imag * real)
            return obj_real * real - obj_imag * imag, obj_real * imag + obj_imag * real

        @pl.when(jnp.logical_not(last))
        def _():
            wave_copy().start()
            copy(back, back_in, send_back, recv_back, partner).wait_recv()
            real, imag = both_sides(back_in[0], back_in[1], right, left_high, left_low)
            back[0], back[1] = step_back(count - 1, real, imag)

        @pl.when(last)
        def _():
            pl.when(core == 0)(lambda: seen_copy().wait_recv())
            end = count - 1
            wave_real, wave_imag = waves[end, 0], waves[end, 1]
            obj_real, obj_imag = win[end, 0], win[end, 1]
            real, imag = both_sides(
                wave_real * obj_real - wave_imag * obj_imag, wave_real * obj_imag + wave_imag * obj_real,
                dft_right, dft_left_high, dft_left_low,
            )
            misfit = 2.0 * (real * real + imag * imag - seen_in[...])
            real, imag = both_sides(
                misfit * real, -(misfit * imag), dft_right, dft_left_high, dft_left_low
            )
            back[0], back[1] = step_back(end, real, imag)

        def hand_out(k):
            canvas[:, width:2 * width] = steps[k]
            own = [canvas[part, pl.ds(width - rows, width), :] for part in range(2)]
            at = k % slab

            @pl.when(k // slab == core)
            def _():
                for part in range(2):
                    mine[at, part] = own[part]

            @pl.when(k // slab != core)
            def _():
                for part in range(2):
                    pair_send[at, part] = own[part]
                grad_copy(at).start()

            @pl.when(split_core)
            def _():
                for part in range(2):
                    spill_out[k, part] = canvas[part, pl.ds(2 * width - rows, width), :]
                spill_copy(k).start()

        real, imag = back[0], back[1]
        for k in reversed(range(count - 1)):
            real, imag = both_sides(real, imag, right, left_high, left_low)
            real, imag = step_back(k, real, imag)
        back[0] = real
        back[1] = imag

        @pl.when(jnp.logical_not(first))
        def _():
            back_copy().start()

        share = width // depth_count

        @pl.when(first)
        def _():
            for k in range(depth_count):
                chunks[k, 0] = back[0, k * share:(k + 1) * share]
                chunks[k, 1] = -back[1, k * share:(k + 1) * share]
            for side in range(2):
                @pl.when(core == side)
                def _():
                    for k in range(depth_count):
                        if k != side:
                            chunk_copy(k, side).start()
                    parts[side] = chunks[side]

        lax.fori_loop(0, count, lambda s, c: (hand_out(count - 1 - s), c)[1], 0)

        def await_chunk(k):
            copy(chunks.at[0], parts.at[k], send_chunk.at[0], recv_chunk.at[k], partner).wait_recv()

        @pl.when(first)
        def _():
            await_chunk(1 - core)

        @pl.when(jnp.logical_not(first))
        def _():
            await_chunk(0)
            await_chunk(1)

        blank = jnp.zeros((width, width), F32)

        def shifted_right(plane, amount):
            return pltpu.roll(jnp.concatenate([plane, blank], 1), amount, 1)

        def add_up(k):
            grad_copy(k).wait_recv()
            copy(spill_out.at[k], spill_in.at[k], send_spill.at[k], recv_spill.at[k], partner).wait_recv()
            for part in range(2):
                grad[k, part] = shifted_right(mine[k, part], col_mine) + shifted_right(pair_in[k, part], col_pair)
                spill_grad[k, part] = shifted_right(spill_in[k, part], col_before)

        value = parts[0] + parts[1]
        base = 0
        for level, clique in enumerate(cliques):
            total[level] = value
            hops = [
                copy(
                    total.at[level], around.at[base + k], send_around.at[base + k],
                    recv_around.at[base + k], device,
                )
                for k, device in enumerate(clique)
            ]
            for hop in hops:
                hop.start()
            for k in range(slab):
                if (level == 0) == (k > 0) or len(cliques) == 1:
                    add_up(k)
            if level == len(cliques) - 1:
                probe_grad[...] = value
                value = jnp.zeros_like(value)
            for k, hop in enumerate(hops):
                hop.wait_recv()
                value = value + around[base + k]
            base += len(clique)
        probe_rest[...] = value

        note_copy().wait_send()
        for k in range(slab):
            pl.when(core == 0)(lambda: early_copy(k).wait_send())
            pl.when(core == 1)(lambda: halo_copy(k).wait_send())
            pair_copy(k).wait_send()
            grad_copy(k).wait_send()

        @pl.when(last & (core == 0))
        def _():
            seen_copy().wait_send()

        @pl.when(split_core)
        def _():
            for k in range(count):
                spill_copy(k).wait_send()

        @pl.when(jnp.logical_not(last))
        def _():
            wave_copy().wait_send()

        @pl.when(jnp.logical_not(first))
        def _():
            back_copy().wait_send()

        @pl.when(first)
        def _():
            for side in range(2):
                @pl.when(core == side)
                def _():
                    for k in range(depth_count):
                        if k != side:
                            chunk_copy(k, side).wait_send()

        base = 0
        for level, clique in enumerate(cliques):
            for k, device in enumerate(clique):
                copy(
                    total.at[level], around.at[base + k], send_around.at[base + k],
                    recv_around.at[base + k], device,
                ).wait_send()
            base += len(clique)

    links = sum(side - 1 for side in sides)
    share = width // depth_count
    plane = (2, width, width)
    buffers = [
        (slab,) + plane, (slab,) + plane, (count,) + plane, (count,) + plane, (2, 2 * width, width),
        (count,) + plane, (count + 1,) + plane, plane, plane, (count,) + plane, (2, 3 * width, width),
        (slab,) + plane, (slab,) + plane, (slab,) + plane, (count,) + plane, (slab,) + plane,
        (width, width), (width, width), (depth_count, 2, share, width), (2, 2, share, width),
        (len(sides), 2, share, width), (links, 2, share, width),
    ]
    dma = pltpu.SemaphoreType.DMA
    marks = [
        dma((slab,)), dma((slab,)), dma, dma, dma((slab,)), dma((count,)), dma, dma((depth_count,)), dma((links,)),
        dma((count,)), dma((slab,)), dma, dma, dma((slab,)), dma((slab,)), dma, dma((2,)), dma((links,)),
    ]
    square = (2 * width, 2 * width)
    tables = [(6 * width, 2 * width), square, square] * 2
    inputs = [(slab, 2, width, 2 * width), plane, plane]
    head = [pltpu.VMEM(shape, BF16) for shape in tables] + [pltpu.VMEM(shape, F32) for shape in inputs]
    head += [pltpu.SMEM((2,), jnp.int32)] * 4
    head += [dma((6,)), dma((slab,)), dma((4,)), dma, dma]
    head += [pltpu.VMEM((early, 2, width, 2 * width), F32)]
    return kernel, head + [pltpu.VMEM(shape, F32) for shape in buffers] + marks


def body(objects, probe, row_offsets, col_offsets, intensity):
    slab = objects.shape[0]
    width = probe.shape[-1]
    depth_count = lax.axis_size("depth")
    scan_count = lax.axis_size("scan")
    kernel, scratch = make_kernel(depth_count, scan_count, slab, width)
    tables = [jnp.asarray(table) for table in transfer_tables(width)]
    vmem = pl.BlockSpec(memory_space=pltpu.VMEM)
    anywhere = pl.BlockSpec(memory_space=pl.ANY)
    share = jax.ShapeDtypeStruct((2, width // depth_count, width), F32)
    tile = jax.ShapeDtypeStruct(objects.shape, F32)
    grad, spill_grad, probe_grad, probe_rest = pl.pallas_call(
        kernel,
        out_shape=(tile, tile, share, share),
        in_specs=[anywhere] * 11,
        out_specs=(vmem, vmem, vmem, vmem),
        scratch_shapes=scratch,
        compiler_params=pltpu.CompilerParams(
            collective_id=0, has_side_effects=True, vmem_limit_bytes=56 << 20
        ),
        name="slices",
    )(row_offsets, col_offsets, objects, probe, intensity, *tables)
    return grad + spill_grad, probe_grad + probe_rest


def solution(mesh):
    in_specs = (P("depth", None, "scan", None), P(), P("scan"), P("scan"), P("scan", None, None))
    out_specs = (P("depth", None, "scan", None), P(None, "depth", None))
    return jax.shard_map(body, mesh=mesh, in_specs=in_specs, out_specs=out_specs, check_vma=False)
```

```python
import jax
import jax.numpy as jnp
import ml_dtypes
import numpy as np
from jax import lax
from jax.experimental import pallas as pl
from jax.experimental.pallas import tpu as pltpu
from jax.sharding import PartitionSpec as P

PROPAGATION = 0.5
F32 = jnp.float32
BF16 = jnp.bfloat16
MESH = pl.DeviceIdType.MESH


def split_table(table):
    high = table.astype(ml_dtypes.bfloat16)
    low = (table - high.astype(np.float64)).astype(ml_dtypes.bfloat16)
    return high, low


def block_tables(matrix):
    real, imag = matrix.real, matrix.imag
    right_high, right_low = split_table(np.block([[real, imag], [-imag, real]]))
    left_high, left_low = split_table(np.block([[real, -imag], [imag, real]]))
    return np.concatenate([right_high, right_high, right_low], 0), left_high, left_low


def transfer_tables(width):
    index = np.arange(width)
    frequency = np.where(index < width // 2, index, index - width).astype(np.float64)
    fourier = np.exp(-2j * np.pi * (np.outer(index, index) % width) / width) / np.sqrt(width)
    chirp = np.exp(-1j * PROPAGATION * np.pi * frequency**2 / width)
    spread = fourier.conj() @ (chirp[:, None] * fourier)
    return block_tables(spread) + block_tables(fourier)


def groups_of(count):
    return [16, count // 16] if count % 16 == 0 and count > 16 else [count]


def split(x):
    high = x.astype(BF16)
    return high, (x - high.astype(F32)).astype(BF16)


def dot(a, b):
    return jnp.dot(a, b, preferred_element_type=F32)


def both_sides(real, imag, right, left_high, left_low):
    width = real.shape[0]
    high, low = split(jnp.concatenate([real, imag], 1))
    mid = dot(jnp.concatenate([high, low, high], 1), right[...])
    high, low = split(jnp.concatenate([mid[:, :width], mid[:, width:]], 0))
    pair = dot(left_high[...], jnp.concatenate([high, low], 1))
    out = pair[:, :width] + pair[:, width:] + dot(left_low[...], high)
    return out[:width], out[width:]


def make_kernel(depth_count, scan_count, slab, width):
    stages = depth_count // 2
    count = 2 * slab
    sides = groups_of(scan_count)
    early = slab

    def kernel(
        row_hbm, col_hbm, objects_hbm, probe_hbm, intensity_hbm, *rest
    ):
        tables_hbm, rest = rest[:6], rest[6:]
        grad, probe_grad, *scratch = rest
        run(row_hbm, col_hbm, objects_hbm, probe_hbm, intensity_hbm, tables_hbm, grad, probe_grad, *scratch)

    def run(
        row_hbm, col_hbm, objects_hbm, probe_hbm, intensity_hbm, tables_hbm, grad, probe_grad,
        right, left_high, left_low, dft_right, dft_left_high, dft_left_low,
        objects, probe, intensity, row_off, col_off, note_out, note_in,
        load_tables, load_objects, load_small, send_note, recv_note,
        sums, store_sums, early_win, far_parts, far_sum, recv_far, send_relay,
        halo_out, pair_out, own_win, halo_win, ext, win, waves, back_in, back, steps, canvas,
        mine, pair_send, pair_in, spill_out, spill_in, seen_out, seen_in, chunks, parts, total, around,
        send_halo, send_pair, send_wave, send_back, send_grad, send_spill, send_seen, send_chunk, send_around,
        recv_halo, recv_pair, recv_wave, recv_back, recv_grad, recv_spill, recv_seen, recv_chunk, recv_around,
    ):
        dep = lax.axis_index("depth")
        me = lax.axis_index("scan")
        stage = dep // 2
        core = dep % 2
        first = stage == 0
        last = stage == stages - 1
        split_core = core == 0
        after = lax.rem(me + 1, scan_count)
        before = lax.rem(me + scan_count - 1, scan_count)
        partner = (dep + 1 - 2 * core, me)
        ahead = lax.rem(stage + 1, stages)
        behind = lax.rem(stage + stages - 1, stages)
        crew = [partner] + [(2 * near + k, me) for near in (ahead, behind) for k in range(2)]
        cliques = []
        stride = 1
        for side in sides:
            place = (me // stride) % side
            cliques.append(
                [(dep, me + (lax.rem(place + k, side) - place) * stride) for k in range(1, side)]
            )
            stride *= side
        friends = crew + [(2 * stage + k, near) for near in (after, before) for k in range(2)]
        for clique in cliques:
            friends = friends + clique

        def copy(source, target, send, recv, device):
            return pltpu.make_async_remote_copy(
                src_ref=source, dst_ref=target, send_sem=send, recv_sem=recv,
                device_id=device, device_id_type=MESH,
            )

        def local(source, target, sem):
            return pltpu.make_async_copy(source, target, sem)

        barrier = pltpu.get_barrier_semaphore()
        for friend in friends:
            pl.semaphore_signal(barrier, inc=1, device_id=friend, device_id_type=MESH)

        loads = [local(row_hbm, row_off, load_small.at[0]), local(col_hbm, col_off, load_small.at[1])]
        object_loads = [local(objects_hbm.at[k], objects.at[k], load_objects.at[k]) for k in range(slab)]
        small_loads = [local(probe_hbm, probe, load_small.at[2]), local(intensity_hbm, intensity, load_small.at[3])]
        tables = [right, left_high, left_low, dft_right, dft_left_high, dft_left_low]
        table_loads = [local(tables_hbm[k], tables[k], load_tables.at[k]) for k in range(6)]
        for load in loads + object_loads + small_loads + table_loads:
            load.start()

        for load in loads:
            load.wait()
        rows_here = [row_off[k] - me * width for k in range(2)]
        second = rows_here[0] != width
        col_split = jnp.where(second, col_off[0], col_off[1])
        col_whole_here = jnp.where(second, col_off[1], col_off[0])
        row_split = jnp.where(second, rows_here[0], rows_here[1])
        rows = jnp.where(split_core, jnp.clip(row_split, 0, width), 0)
        note_out[0] = col_whole_here
        note_out[1] = col_split

        def note_copy():
            return copy(note_out, note_in, send_note, recv_note, (dep, after))

        def halo_copy(k):
            return copy(
                halo_out.at[k], halo_win.at[slab * core + k], send_halo.at[k],
                recv_halo.at[slab * core + k], (2 * stage, before),
            )

        def early_copy(k):
            return copy(
                objects.at[k], early_win.at[k], send_halo.at[k], recv_halo.at[k], (2 * stage, before)
            )

        def pair_copy(k):
            return copy(
                pair_out.at[k], own_win.at[slab * core + k], send_pair.at[k], recv_pair.at[k], partner
            )

        def seen_copy():
            return copy(seen_out, seen_in, send_seen, recv_seen, (dep, after))

        def wave_copy():
            return copy(waves.at[count], waves.at[0], send_wave, recv_wave, (dep + 2, me))

        def back_copy():
            return copy(back, back_in, send_back, recv_back, (dep - 2, me))

        def grad_copy(k):
            return copy(pair_send.at[k], pair_in.at[k], send_grad.at[k], recv_grad.at[k], partner)

        def spill_copy(k):
            return copy(
                spill_out.at[k], spill_in.at[k % slab], send_spill.at[k], recv_spill.at[k % slab],
                (2 * stage + k // slab, after),
            )

        def chunk_copy(target, core_from):
            if False:
                way = 2 if target % 2 == 0 else 7
                return copy(
                    chunks.at[target], far_parts.at[core_from], send_chunk.at[target], recv_far.at[core_from], (way, me)
                )
            return copy(
                chunks.at[target], parts.at[core_from], send_chunk.at[target], recv_chunk.at[core_from], (target, me)
            )

        def relay_copy():
            target = jnp.where(dep == 2, 4, 5)
            return copy(far_sum, parts.at[0], send_relay, recv_chunk.at[0], (target, me))

        def shifted_left(plane, amount):
            return pltpu.roll(plane, lax.rem(2 * width - amount, 2 * width), 1)[:, :width]

        for k in range(slab):
            object_loads[k].wait()
            for part in range(2):
                window = shifted_left(objects[k, part], col_split)

                @pl.when(split_core)
                def _():
                    own_win[k, part] = window

                @pl.when(jnp.logical_not(split_core))
                def _():
                    pair_out[k, part] = window

        pl.semaphore_wait(barrier, len(friends))
        note_copy().start()

        @pl.when(split_core)
        def _():
            for k in range(early):
                early_copy(k).start()

        @pl.when(jnp.logical_not(split_core))
        def _():
            for k in range(slab):
                pair_copy(k).start()

        ext[...] = jnp.zeros_like(ext)
        canvas[...] = jnp.zeros_like(canvas)
        note_copy().wait_recv()
        col_whole = note_in[0]
        col_before = note_in[1]
        col_mine = jnp.where(split_core, col_split, col_whole)
        col_pair = jnp.where(split_core, col_whole, col_split)

        for k in range(slab):
            for part in range(2):
                window = shifted_left(objects[k, part], col_whole)

                @pl.when(split_core)
                def _():
                    pair_out[k, part] = window

                @pl.when(jnp.logical_not(split_core))
                def _():
                    own_win[slab + k, part] = window

            @pl.when(split_core)
            def _():
                pair_copy(k).start()

        for k in range(slab):
            def send_window():
                for part in range(2):
                    halo_out[k, part] = shifted_left(objects[k, part], col_before)
                halo_copy(k).start()

            if k < early:
                pl.when(jnp.logical_not(split_core))(send_window)
            else:
                send_window()

        for load in small_loads + table_loads:
            load.wait()
        measured_split = jnp.where(second, intensity[0], intensity[1])
        measured_whole = jnp.where(second, intensity[1], intensity[0])

        @pl.when(last & (core == 1))
        def _():
            seen_out[...] = measured_whole
            seen_copy().start()

        @pl.when(split_core)
        def _():
            seen_in[...] = measured_split

        def gather_window(k):
            @pl.when(core != k // slab)
            def _():
                copy(
                    pair_out.at[k % slab], own_win.at[k], send_pair.at[k % slab],
                    recv_pair.at[k % slab], partner,
                ).wait_recv()

            @pl.when(split_core)
            def _():
                if k < early:
                    early_copy(k).wait_recv()
                    for part in range(2):
                        ext[part, width:] = shifted_left(early_win[k, part], col_split)
                else:
                    copy(
                        halo_out.at[k % slab], halo_win.at[k], send_halo.at[k % slab],
                        recv_halo.at[k], partner,
                    ).wait_recv()
                    ext[:, width:] = halo_win[k]

            ext[:, :width] = own_win[k]
            for part in range(2):
                win[k, part] = ext[part, pl.ds(rows, width), :]

        def forward(k, real, imag):
            obj_real, obj_imag = win[k, 0], win[k, 1]
            real, imag = both_sides(
                real * obj_real - imag * obj_imag, real * obj_imag + imag * obj_real,
                right, left_high, left_low,
            )
            waves[k + 1, 0] = real
            waves[k + 1, 1] = imag
            return real, imag

        @pl.when(first)
        def _():
            waves[0] = probe[...]
            for k in range(count):
                gather_window(k)
                forward(k, waves[k, 0], waves[k, 1])

        @pl.when(jnp.logical_not(first))
        def _():
            for k in range(count):
                gather_window(k)
            wave_copy().wait_recv()
            real, imag = waves[0, 0], waves[0, 1]
            for k in range(count - 1):
                real, imag = forward(k, real, imag)

            @pl.when(jnp.logical_not(last))
            def _():
                forward(count - 1, real, imag)

        def step_back(k, real, imag):
            wave_real, wave_imag = waves[k, 0], waves[k, 1]
            obj_real, obj_imag = win[k, 0], win[k, 1]
            steps[k, 0] = wave_real * real - wave_imag * imag
            steps[k, 1] = -(wave_real * imag + wave_imag * real)
            return obj_real * real - obj_imag * imag, obj_real * imag + obj_imag * real

        @pl.when(jnp.logical_not(last))
        def _():
            wave_copy().start()
            copy(back, back_in, send_back, recv_back, partner).wait_recv()
            real, imag = both_sides(back_in[0], back_in[1], right, left_high, left_low)
            back[0], back[1] = step_back(count - 1, real, imag)

        @pl.when(last)
        def _():
            pl.when(core == 1)(lambda: seen_copy().wait_recv())
            end = count - 1
            wave_real, wave_imag = waves[end, 0], waves[end, 1]
            obj_real, obj_imag = win[end, 0], win[end, 1]
            real, imag = both_sides(
                wave_real * obj_real - wave_imag * obj_imag, wave_real * obj_imag + wave_imag * obj_real,
                dft_right, dft_left_high, dft_left_low,
            )
            misfit = 2.0 * (real * real + imag * imag - seen_in[...])
            real, imag = both_sides(
                misfit * real, -(misfit * imag), dft_right, dft_left_high, dft_left_low
            )
            back[0], back[1] = step_back(end, real, imag)

        def hand_out(k):
            canvas[:, width:2 * width] = steps[k]
            own = [canvas[part, pl.ds(width - rows, width), :] for part in range(2)]
            at = k % slab

            @pl.when(k // slab == core)
            def _():
                for part in range(2):
                    mine[at, part] = own[part]

            @pl.when(k // slab != core)
            def _():
                for part in range(2):
                    pair_send[at, part] = own[part]
                grad_copy(at).start()

            @pl.when(split_core)
            def _():
                for part in range(2):
                    spill_out[k, part] = canvas[part, pl.ds(2 * width - rows, width), :]
                spill_copy(k).start()

        real, imag = back[0], back[1]
        for k in reversed(range(count - 1)):
            real, imag = both_sides(real, imag, right, left_high, left_low)
            real, imag = step_back(k, real, imag)
        back[0] = real
        back[1] = imag

        @pl.when(jnp.logical_not(first))
        def _():
            back_copy().start()

        share = width // depth_count

        @pl.when(first)
        def _():
            for k in range(depth_count):
                chunks[k, 0] = back[0, k * share:(k + 1) * share]
                chunks[k, 1] = -back[1, k * share:(k + 1) * share]
            for side in range(2):
                @pl.when(core == side)
                def _():
                    for k in range(depth_count):
                        if k != side:
                            chunk_copy(k, side).start()
                    parts[side] = chunks[side]

        lax.fori_loop(0, count, lambda s, c: (hand_out(count - 1 - s), c)[1], 0)

        def await_chunk(k):
            copy(chunks.at[0], parts.at[k], send_chunk.at[0], recv_chunk.at[k], partner).wait_recv()

        if False:
            @pl.when((dep == 2) | (dep == 7))
            def _():
                for k in range(2):
                    copy(chunks.at[0], far_parts.at[k], send_chunk.at[0], recv_far.at[k], partner).wait_recv()
                far_sum[...] = far_parts[0] + far_parts[1]
                relay_copy().start()

        @pl.when(first)
        def _():
            await_chunk(1 - core)

        @pl.when(jnp.logical_not(first))
        def _():
            await_chunk(0)
            await_chunk(1)

        blank = jnp.zeros((width, width), F32)

        def shifted_right(plane, amount):
            return pltpu.roll(jnp.concatenate([plane, blank], 1), amount, 1)

        def add_up(k):
            grad_copy(k).wait_recv()
            copy(spill_out.at[k], spill_in.at[k], send_spill.at[k], recv_spill.at[k], partner).wait_recv()
            for part in range(2):
                sums[k, part] = (
                    shifted_right(mine[k, part], col_mine)
                    + shifted_right(pair_in[k, part], col_pair)
                    + shifted_right(spill_in[k, part], col_before)
                )
            local(sums.at[k], grad.at[k], store_sums.at[k]).start()

        value = parts[0] + parts[1]
        base = 0
        for level, clique in enumerate(cliques):
            total[level] = value
            hops = [
                copy(
                    total.at[level], around.at[base + k], send_around.at[base + k],
                    recv_around.at[base + k], device,
                )
                for k, device in enumerate(clique)
            ]
            for hop in hops:
                hop.start()
            for k in range(slab):
                if (level == 0) == (k > 0) or len(cliques) == 1:
                    add_up(k)
            for k, hop in enumerate(hops):
                hop.wait_recv()
                value = value + around[base + k]
            base += len(clique)
        probe_grad[...] = value

        note_copy().wait_send()
        for k in range(slab):
            local(sums.at[k], grad.at[k], store_sums.at[k]).wait()
            if k < early:
                pl.when(split_core)(lambda: early_copy(k).wait_send())
                pl.when(jnp.logical_not(split_core))(lambda: halo_copy(k).wait_send())
            else:
                halo_copy(k).wait_send()
            pair_copy(k).wait_send()
            grad_copy(k).wait_send()

        @pl.when(last & (core == 1))
        def _():
            seen_copy().wait_send()

        @pl.when(split_core)
        def _():
            for k in range(count):
                spill_copy(k).wait_send()

        @pl.when(jnp.logical_not(last))
        def _():
            wave_copy().wait_send()

        @pl.when(jnp.logical_not(first))
        def _():
            back_copy().wait_send()

        @pl.when(first)
        def _():
            for side in range(2):
                @pl.when(core == side)
                def _():
                    for k in range(depth_count):
                        if k != side:
                            chunk_copy(k, side).wait_send()

        if False:
            @pl.when((dep == 2) | (dep == 7))
            def _():
                relay_copy().wait_send()

        base = 0
        for level, clique in enumerate(cliques):
            for k, device in enumerate(clique):
                copy(
                    total.at[level], around.at[base + k], send_around.at[base + k],
                    recv_around.at[base + k], device,
                ).wait_send()
            base += len(clique)

    links = sum(side - 1 for side in sides)
    share = width // depth_count
    plane = (2, width, width)
    buffers = [
        (slab,) + plane, (slab,) + plane, (count,) + plane, (count,) + plane, (2, 2 * width, width),
        (count,) + plane, (count + 1,) + plane, plane, plane, (count,) + plane, (2, 3 * width, width),
        (slab,) + plane, (slab,) + plane, (slab,) + plane, (count,) + plane, (slab,) + plane,
        (width, width), (width, width), (depth_count, 2, share, width), (2, 2, share, width),
        (len(sides), 2, share, width), (links, 2, share, width),
    ]
    dma = pltpu.SemaphoreType.DMA
    marks = [
        dma((slab,)), dma((slab,)), dma, dma, dma((slab,)), dma((count,)), dma, dma((depth_count,)), dma((links,)),
        dma((count,)), dma((slab,)), dma, dma, dma((slab,)), dma((slab,)), dma, dma((2,)), dma((links,)),
    ]
    square = (2 * width, 2 * width)
    tables = [(6 * width, 2 * width), square, square] * 2
    inputs = [(slab, 2, width, 2 * width), plane, plane]
    head = [pltpu.VMEM(shape, BF16) for shape in tables] + [pltpu.VMEM(shape, F32) for shape in inputs]
    head += [pltpu.SMEM((2,), jnp.int32)] * 4
    head += [dma((6,)), dma((slab,)), dma((4,)), dma, dma]
    piece = (2, share, width)
    head += [pltpu.VMEM((slab, 2, width, 2 * width), F32), dma((slab,))]
    head += [pltpu.VMEM((early, 2, width, 2 * width), F32), pltpu.VMEM((2,) + piece, F32), pltpu.VMEM(piece, F32)]
    head += [dma((2,)), dma]
    return kernel, head + [pltpu.VMEM(shape, F32) for shape in buffers] + marks


def body(objects, probe, row_offsets, col_offsets, intensity):
    slab = objects.shape[0]
    width = probe.shape[-1]
    depth_count = lax.axis_size("depth")
    scan_count = lax.axis_size("scan")
    kernel, scratch = make_kernel(depth_count, scan_count, slab, width)
    tables = [jnp.asarray(table) for table in transfer_tables(width)]
    vmem = pl.BlockSpec(memory_space=pltpu.VMEM)
    anywhere = pl.BlockSpec(memory_space=pl.ANY)
    return pl.pallas_call(
        kernel,
        out_shape=(
            jax.ShapeDtypeStruct(objects.shape, F32),
            jax.ShapeDtypeStruct((2, width // depth_count, width), F32),
        ),
        in_specs=[anywhere] * 11,
        out_specs=(anywhere, vmem),
        scratch_shapes=scratch,
        compiler_params=pltpu.CompilerParams(
            collective_id=0, has_side_effects=True, vmem_limit_bytes=56 << 20
        ),
        name="slices",
    )(row_offsets, col_offsets, objects, probe, intensity, *tables)


def solution(mesh):
    in_specs = (P("depth", None, "scan", None), P(), P("scan"), P("scan"), P("scan", None, None))
    out_specs = (P("depth", None, "scan", None), P(None, "depth", None))
    return jax.shard_map(body, mesh=mesh, in_specs=in_specs, out_specs=out_specs, check_vma=False)
```

```python
import jax
import jax.numpy as jnp
import ml_dtypes
import numpy as np
from jax import lax
from jax.experimental import pallas as pl
from jax.experimental.pallas import tpu as pltpu
from jax.sharding import PartitionSpec as P

PROPAGATION = 0.5
F32 = jnp.float32
BF16 = jnp.bfloat16
MESH = pl.DeviceIdType.MESH


def split_table(table):
    high = table.astype(ml_dtypes.bfloat16)
    low = (table - high.astype(np.float64)).astype(ml_dtypes.bfloat16)
    return high, low


def block_tables(matrix):
    real, imag = matrix.real, matrix.imag
    right_high, right_low = split_table(np.block([[real, imag], [-imag, real]]))
    left_high, left_low = split_table(np.block([[real, -imag], [imag, real]]))
    return np.concatenate([right_high, right_high, right_low], 0), left_high, left_low


def transfer_tables(width):
    index = np.arange(width)
    frequency = np.where(index < width // 2, index, index - width).astype(np.float64)
    fourier = np.exp(-2j * np.pi * (np.outer(index, index) % width) / width) / np.sqrt(width)
    chirp = np.exp(-1j * PROPAGATION * np.pi * frequency**2 / width)
    spread = fourier.conj() @ (chirp[:, None] * fourier)
    return block_tables(spread) + block_tables(fourier)


def groups_of(count):
    return [16, count // 16] if count % 16 == 0 and count > 16 else [count]


def split(x):
    high = x.astype(BF16)
    return high, (x - high.astype(F32)).astype(BF16)


def dot(a, b):
    return jnp.dot(a, b, preferred_element_type=F32)


def both_sides(real, imag, right, left_high, left_low):
    width = real.shape[0]
    high, low = split(jnp.concatenate([real, imag], 1))
    mid = dot(jnp.concatenate([high, low, high], 1), right[...])
    high, low = split(jnp.concatenate([mid[:, :width], mid[:, width:]], 0))
    pair = dot(left_high[...], jnp.concatenate([high, low], 1))
    out = pair[:, :width] + pair[:, width:] + dot(left_low[...], high)
    return out[:width], out[width:]


def make_kernel(depth_count, scan_count, slab, width):
    stages = depth_count // 2
    count = 2 * slab
    sides = groups_of(scan_count)
    early = slab

    def kernel(
        row_hbm, col_hbm, objects_hbm, probe_hbm, intensity_hbm, *rest
    ):
        tables_hbm, rest = rest[:6], rest[6:]
        grad, probe_grad, *scratch = rest
        run(row_hbm, col_hbm, objects_hbm, probe_hbm, intensity_hbm, tables_hbm, grad, probe_grad, *scratch)

    def run(
        row_hbm, col_hbm, objects_hbm, probe_hbm, intensity_hbm, tables_hbm, grad, probe_grad,
        right, left_high, left_low, dft_right, dft_left_high, dft_left_low,
        objects, probe, intensity, row_off, col_off, note_out, note_in,
        load_tables, load_objects, load_small, send_note, recv_note,
        sums, store_sums, early_win, far_parts, far_sum, recv_far, send_relay,
        halo_out, pair_out, own_win, halo_win, ext, win, waves, back_in, back, steps, canvas,
        mine, pair_send, pair_in, spill_out, spill_in, seen_out, seen_in, chunks, parts, total, around,
        send_halo, send_pair, send_wave, send_back, send_grad, send_spill, send_seen, send_chunk, send_around,
        recv_halo, recv_pair, recv_wave, recv_back, recv_grad, recv_spill, recv_seen, recv_chunk, recv_around,
    ):
        dep = lax.axis_index("depth")
        me = lax.axis_index("scan")
        stage = dep // 2
        core = dep % 2
        first = stage == 0
        last = stage == stages - 1
        split_core = core == 0
        after = lax.rem(me + 1, scan_count)
        before = lax.rem(me + scan_count - 1, scan_count)
        partner = (dep + 1 - 2 * core, me)
        ahead = lax.rem(stage + 1, stages)
        behind = lax.rem(stage + stages - 1, stages)
        crew = [partner] + [(2 * near + k, me) for near in (ahead, behind) for k in range(2)]
        cliques = []
        stride = 1
        for side in sides:
            place = (me // stride) % side
            cliques.append(
                [(dep, me + (lax.rem(place + k, side) - place) * stride) for k in range(1, side)]
            )
            stride *= side
        friends = crew + [(2 * stage + k, near) for near in (after, before) for k in range(2)]
        for clique in cliques:
            friends = friends + clique

        def copy(source, target, send, recv, device):
            return pltpu.make_async_remote_copy(
                src_ref=source, dst_ref=target, send_sem=send, recv_sem=recv,
                device_id=device, device_id_type=MESH,
            )

        def local(source, target, sem):
            return pltpu.make_async_copy(source, target, sem)

        barrier = pltpu.get_barrier_semaphore()
        for friend in friends:
            pl.semaphore_signal(barrier, inc=1, device_id=friend, device_id_type=MESH)

        loads = [local(row_hbm, row_off, load_small.at[0]), local(col_hbm, col_off, load_small.at[1])]
        object_loads = [local(objects_hbm.at[k], objects.at[k], load_objects.at[k]) for k in range(slab)]
        small_loads = [local(probe_hbm, probe, load_small.at[2]), local(intensity_hbm, intensity, load_small.at[3])]
        tables = [right, left_high, left_low, dft_right, dft_left_high, dft_left_low]
        table_loads = [local(tables_hbm[k], tables[k], load_tables.at[k]) for k in range(6)]
        for load in loads + object_loads + small_loads + table_loads:
            load.start()

        for load in loads:
            load.wait()
        rows_here = [row_off[k] - me * width for k in range(2)]
        second = rows_here[0] != width
        col_split = jnp.where(second, col_off[0], col_off[1])
        col_whole_here = jnp.where(second, col_off[1], col_off[0])
        row_split = jnp.where(second, rows_here[0], rows_here[1])
        rows = jnp.where(split_core, jnp.clip(row_split, 0, width), 0)
        note_out[0] = col_whole_here
        note_out[1] = col_split

        def note_copy():
            return copy(note_out, note_in, send_note, recv_note, (dep, after))

        def halo_copy(k):
            return copy(
                halo_out.at[k], halo_win.at[slab * core + k], send_halo.at[k],
                recv_halo.at[slab * core + k], (2 * stage, before),
            )

        def early_copy(k):
            return copy(
                objects.at[k], early_win.at[k], send_halo.at[k], recv_halo.at[k], (2 * stage, before)
            )

        def pair_copy(k):
            return copy(
                pair_out.at[k], own_win.at[slab * core + k], send_pair.at[k], recv_pair.at[k], partner
            )

        def seen_copy():
            return copy(seen_out, seen_in, send_seen, recv_seen, (dep, after))

        def wave_copy():
            return copy(waves.at[count], waves.at[0], send_wave, recv_wave, (dep + 2, me))

        def back_copy():
            return copy(back, back_in, send_back, recv_back, (dep - 2, me))

        def grad_copy(k):
            return copy(pair_send.at[k], pair_in.at[k], send_grad.at[k], recv_grad.at[k], partner)

        def spill_copy(k):
            return copy(
                spill_out.at[k], spill_in.at[k % slab], send_spill.at[k], recv_spill.at[k % slab],
                (2 * stage + k // slab, after),
            )

        def chunk_copy(target, core_from):
            if False:
                way = 2 if target % 2 == 0 else 7
                return copy(
                    chunks.at[target], far_parts.at[core_from], send_chunk.at[target], recv_far.at[core_from], (way, me)
                )
            return copy(
                chunks.at[target], parts.at[core_from], send_chunk.at[target], recv_chunk.at[core_from], (target, me)
            )

        def relay_copy():
            target = jnp.where(dep == 2, 4, 5)
            return copy(far_sum, parts.at[0], send_relay, recv_chunk.at[0], (target, me))

        def shifted_left(plane, amount):
            return pltpu.roll(plane, lax.rem(2 * width - amount, 2 * width), 1)[:, :width]

        for k in range(slab):
            object_loads[k].wait()
            for part in range(2):
                window = shifted_left(objects[k, part], col_split)

                @pl.when(split_core)
                def _():
                    own_win[k, part] = window

                @pl.when(jnp.logical_not(split_core))
                def _():
                    pair_out[k, part] = window

        pl.semaphore_wait(barrier, len(friends))
        note_copy().start()

        @pl.when(split_core)
        def _():
            for k in range(early):
                early_copy(k).start()

        @pl.when(jnp.logical_not(split_core))
        def _():
            for k in range(slab):
                pair_copy(k).start()

        ext[...] = jnp.zeros_like(ext)
        canvas[...] = jnp.zeros_like(canvas)
        note_copy().wait_recv()
        col_whole = note_in[0]
        col_before = note_in[1]
        col_mine = jnp.where(split_core, col_split, col_whole)
        col_pair = jnp.where(split_core, col_whole, col_split)

        for k in range(slab):
            for part in range(2):
                window = shifted_left(objects[k, part], col_whole)

                @pl.when(split_core)
                def _():
                    pair_out[k, part] = window

                @pl.when(jnp.logical_not(split_core))
                def _():
                    own_win[slab + k, part] = window

            @pl.when(split_core)
            def _():
                pair_copy(k).start()

        for k in range(slab):
            def send_window():
                for part in range(2):
                    halo_out[k, part] = shifted_left(objects[k, part], col_before)
                halo_copy(k).start()

            if k < early:
                pl.when(jnp.logical_not(split_core))(send_window)
            else:
                send_window()

        for load in small_loads + table_loads:
            load.wait()
        measured_split = jnp.where(second, intensity[0], intensity[1])
        measured_whole = jnp.where(second, intensity[1], intensity[0])

        @pl.when(last & (core == 1))
        def _():
            seen_out[...] = measured_whole
            seen_copy().start()

        @pl.when(split_core)
        def _():
            seen_in[...] = measured_split

        def gather_window(k):
            @pl.when(core != k // slab)
            def _():
                copy(
                    pair_out.at[k % slab], own_win.at[k], send_pair.at[k % slab],
                    recv_pair.at[k % slab], partner,
                ).wait_recv()

            @pl.when(split_core)
            def _():
                if k < early:
                    early_copy(k).wait_recv()
                    for part in range(2):
                        ext[part, width:] = shifted_left(early_win[k, part], col_split)
                else:
                    copy(
                        halo_out.at[k % slab], halo_win.at[k], send_halo.at[k % slab],
                        recv_halo.at[k], partner,
                    ).wait_recv()
                    ext[:, width:] = halo_win[k]

            ext[:, :width] = own_win[k]
            for part in range(2):
                win[k, part] = ext[part, pl.ds(rows, width), :]

        def forward(k, real, imag):
            obj_real, obj_imag = win[k, 0], win[k, 1]
            real, imag = both_sides(
                real * obj_real - imag * obj_imag, real * obj_imag + imag * obj_real,
                right, left_high, left_low,
            )
            waves[k + 1, 0] = real
            waves[k + 1, 1] = imag
            return real, imag

        @pl.when(first)
        def _():
            waves[0] = probe[...]
            for k in range(count):
                gather_window(k)
                forward(k, waves[k, 0], waves[k, 1])

        @pl.when(jnp.logical_not(first))
        def _():
            for k in range(count):
                gather_window(k)
            wave_copy().wait_recv()
            real, imag = waves[0, 0], waves[0, 1]
            for k in range(count - 1):
                real, imag = forward(k, real, imag)

            @pl.when(jnp.logical_not(last))
            def _():
                forward(count - 1, real, imag)

        def step_back(k, real, imag):
            wave_real, wave_imag = waves[k, 0], waves[k, 1]
            obj_real, obj_imag = win[k, 0], win[k, 1]
            steps[k, 0] = wave_real * real - wave_imag * imag
            steps[k, 1] = -(wave_real * imag + wave_imag * real)
            return obj_real * real - obj_imag * imag, obj_real * imag + obj_imag * real

        @pl.when(jnp.logical_not(last))
        def _():
            wave_copy().start()
            copy(back, back_in, send_back, recv_back, partner).wait_recv()
            real, imag = both_sides(back_in[0], back_in[1], right, left_high, left_low)
            back[0], back[1] = step_back(count - 1, real, imag)

        @pl.when(last)
        def _():
            pl.when(core == 1)(lambda: seen_copy().wait_recv())
            end = count - 1
            wave_real, wave_imag = waves[end, 0], waves[end, 1]
            obj_real, obj_imag = win[end, 0], win[end, 1]
            real, imag = both_sides(
                wave_real * obj_real - wave_imag * obj_imag, wave_real * obj_imag + wave_imag * obj_real,
                dft_right, dft_left_high, dft_left_low,
            )
            misfit = 2.0 * (real * real + imag * imag - seen_in[...])
            real, imag = both_sides(
                misfit * real, -(misfit * imag), dft_right, dft_left_high, dft_left_low
            )
            back[0], back[1] = step_back(end, real, imag)

        def hand_out(k):
            canvas[:, width:2 * width] = steps[k]
            own = [canvas[part, pl.ds(width - rows, width), :] for part in range(2)]
            at = k % slab

            @pl.when(k // slab == core)
            def _():
                for part in range(2):
                    mine[at, part] = own[part]

            @pl.when(k // slab != core)
            def _():
                for part in range(2):
                    pair_send[at, part] = own[part]
                grad_copy(at).start()

            @pl.when(split_core)
            def _():
                for part in range(2):
                    spill_out[k, part] = canvas[part, pl.ds(2 * width - rows, width), :]
                spill_copy(k).start()

        real, imag = back[0], back[1]
        for k in reversed(range(count - 1)):
            real, imag = both_sides(real, imag, right, left_high, left_low)
            real, imag = step_back(k, real, imag)
        back[0] = real
        back[1] = imag

        @pl.when(jnp.logical_not(first))
        def _():
            back_copy().start()

        share = width // depth_count

        @pl.when(first)
        def _():
            for k in range(depth_count):
                chunks[k, 0] = back[0, k * share:(k + 1) * share]
                chunks[k, 1] = -back[1, k * share:(k + 1) * share]
            for side in range(2):
                @pl.when(core == side)
                def _():
                    for k in range(depth_count):
                        if k != side:
                            chunk_copy(k, side).start()
                    parts[side] = chunks[side]

        lax.fori_loop(0, count, lambda s, c: (hand_out(count - 1 - s), c)[1], 0)

        def await_chunk(k):
            copy(chunks.at[0], parts.at[k], send_chunk.at[0], recv_chunk.at[k], partner).wait_recv()

        if False:
            @pl.when((dep == 2) | (dep == 7))
            def _():
                for k in range(2):
                    copy(chunks.at[0], far_parts.at[k], send_chunk.at[0], recv_far.at[k], partner).wait_recv()
                far_sum[...] = far_parts[0] + far_parts[1]
                relay_copy().start()

        @pl.when(first)
        def _():
            await_chunk(1 - core)

        @pl.when(jnp.logical_not(first))
        def _():
            await_chunk(0)
            await_chunk(1)

        blank = jnp.zeros((width, width), F32)

        def shifted_right(plane, amount):
            return pltpu.roll(jnp.concatenate([plane, blank], 1), amount, 1)

        def add_up(k):
            grad_copy(k).wait_recv()
            copy(spill_out.at[k], spill_in.at[k], send_spill.at[k], recv_spill.at[k], partner).wait_recv()
            for part in range(2):
                grad[k, part] = (
                    shifted_right(mine[k, part], col_mine)
                    + shifted_right(pair_in[k, part], col_pair)
                    + shifted_right(spill_in[k, part], col_before)
                )

        value = parts[0] + parts[1]
        base = 0
        for level, clique in enumerate(cliques):
            total[level] = value
            hops = [
                copy(
                    total.at[level], around.at[base + k], send_around.at[base + k],
                    recv_around.at[base + k], device,
                )
                for k, device in enumerate(clique)
            ]
            for hop in hops:
                hop.start()
            for k in range(slab):
                if (level == 0) == (k > 0) or len(cliques) == 1:
                    add_up(k)
            for k, hop in enumerate(hops):
                hop.wait_recv()
                value = value + around[base + k]
            base += len(clique)
        probe_grad[...] = value

        note_copy().wait_send()
        for k in range(slab):
            if k < early:
                pl.when(split_core)(lambda: early_copy(k).wait_send())
                pl.when(jnp.logical_not(split_core))(lambda: halo_copy(k).wait_send())
            else:
                halo_copy(k).wait_send()
            pair_copy(k).wait_send()
            grad_copy(k).wait_send()

        @pl.when(last & (core == 1))
        def _():
            seen_copy().wait_send()

        @pl.when(split_core)
        def _():
            for k in range(count):
                spill_copy(k).wait_send()

        @pl.when(jnp.logical_not(last))
        def _():
            wave_copy().wait_send()

        @pl.when(jnp.logical_not(first))
        def _():
            back_copy().wait_send()

        @pl.when(first)
        def _():
            for side in range(2):
                @pl.when(core == side)
                def _():
                    for k in range(depth_count):
                        if k != side:
                            chunk_copy(k, side).wait_send()

        if False:
            @pl.when((dep == 2) | (dep == 7))
            def _():
                relay_copy().wait_send()

        base = 0
        for level, clique in enumerate(cliques):
            for k, device in enumerate(clique):
                copy(
                    total.at[level], around.at[base + k], send_around.at[base + k],
                    recv_around.at[base + k], device,
                ).wait_send()
            base += len(clique)

    links = sum(side - 1 for side in sides)
    share = width // depth_count
    plane = (2, width, width)
    buffers = [
        (slab,) + plane, (slab,) + plane, (count,) + plane, (count,) + plane, (2, 2 * width, width),
        (count,) + plane, (count + 1,) + plane, plane, plane, (count,) + plane, (2, 3 * width, width),
        (slab,) + plane, (slab,) + plane, (slab,) + plane, (count,) + plane, (slab,) + plane,
        (width, width), (width, width), (depth_count, 2, share, width), (2, 2, share, width),
        (len(sides), 2, share, width), (links, 2, share, width),
    ]
    dma = pltpu.SemaphoreType.DMA
    marks = [
        dma((slab,)), dma((slab,)), dma, dma, dma((slab,)), dma((count,)), dma, dma((depth_count,)), dma((links,)),
        dma((count,)), dma((slab,)), dma, dma, dma((slab,)), dma((slab,)), dma, dma((2,)), dma((links,)),
    ]
    square = (2 * width, 2 * width)
    tables = [(6 * width, 2 * width), square, square] * 2
    inputs = [(slab, 2, width, 2 * width), plane, plane]
    head = [pltpu.VMEM(shape, BF16) for shape in tables] + [pltpu.VMEM(shape, F32) for shape in inputs]
    head += [pltpu.SMEM((2,), jnp.int32)] * 4
    head += [dma((6,)), dma((slab,)), dma((4,)), dma, dma]
    piece = (2, share, width)
    head += [pltpu.VMEM((slab, 2, width, 2 * width), F32), dma((slab,))]
    head += [pltpu.VMEM((early, 2, width, 2 * width), F32), pltpu.VMEM((2,) + piece, F32), pltpu.VMEM(piece, F32)]
    head += [dma((2,)), dma]
    return kernel, head + [pltpu.VMEM(shape, F32) for shape in buffers] + marks


def body(objects, probe, row_offsets, col_offsets, intensity):
    slab = objects.shape[0]
    width = probe.shape[-1]
    depth_count = lax.axis_size("depth")
    scan_count = lax.axis_size("scan")
    kernel, scratch = make_kernel(depth_count, scan_count, slab, width)
    tables = [jnp.asarray(table) for table in transfer_tables(width)]
    vmem = pl.BlockSpec(memory_space=pltpu.VMEM)
    anywhere = pl.BlockSpec(memory_space=pl.ANY)
    held = pl.pallas_call(
        kernel,
        out_shape=(
            pltpu.VMEM(objects.shape, F32),
            pltpu.VMEM((2, width // depth_count, width), F32),
        ),
        in_specs=[anywhere] * 11,
        out_specs=(vmem, vmem),
        scratch_shapes=scratch,
        compiler_params=pltpu.CompilerParams(
            collective_id=0, has_side_effects=True, vmem_limit_bytes=56 << 20
        ),
        name="slices",
    )(row_offsets, col_offsets, objects, probe, intensity, *tables)

    def store(grad, probe_grad, grad_hbm, probe_grad_hbm, marks):
        moves = [pltpu.make_async_copy(grad.at[k], grad_hbm.at[k], marks.at[k]) for k in range(slab)]
        moves.append(pltpu.make_async_copy(probe_grad, probe_grad_hbm, marks.at[slab]))
        for move in moves:
            move.start()
        for move in moves:
            move.wait()

    return pl.pallas_call(
        store,
        out_shape=tuple(jax.ShapeDtypeStruct(part.shape, F32) for part in held),
        in_specs=[pl.BlockSpec(memory_space=pltpu.VMEM)] * 2,
        compiler_params=pltpu.CompilerParams(vmem_limit_bytes=1 << 20),
        out_specs=(anywhere, anywhere),
        scratch_shapes=[pltpu.SemaphoreType.DMA((slab + 1,))],
        name="store",
    )(*held)


def solution(mesh):
    in_specs = (P("depth", None, "scan", None), P(), P("scan"), P("scan"), P("scan", None, None))
    out_specs = (P("depth", None, "scan", None), P(None, "depth", None))
    return jax.shard_map(body, mesh=mesh, in_specs=in_specs, out_specs=out_specs, check_vma=False)
```

```python
import jax
import jax.numpy as jnp
import ml_dtypes
import numpy as np
from jax import lax
from jax.experimental import pallas as pl
from jax.experimental.pallas import tpu as pltpu
from jax.sharding import PartitionSpec as P

PROPAGATION = 0.5
F32 = jnp.float32
BF16 = jnp.bfloat16
MESH = pl.DeviceIdType.MESH


def split_table(table):
    high = table.astype(ml_dtypes.bfloat16)
    low = (table - high.astype(np.float64)).astype(ml_dtypes.bfloat16)
    return high, low


def block_tables(matrix):
    real, imag = matrix.real, matrix.imag
    right_high, right_low = split_table(np.block([[real, imag], [-imag, real]]))
    left_high, left_low = split_table(np.block([[real, -imag], [imag, real]]))
    return np.concatenate([right_high, right_high, right_low], 0), left_high, left_low


def transfer_tables(width):
    index = np.arange(width)
    frequency = np.where(index < width // 2, index, index - width).astype(np.float64)
    fourier = np.exp(-2j * np.pi * (np.outer(index, index) % width) / width) / np.sqrt(width)
    chirp = np.exp(-1j * PROPAGATION * np.pi * frequency**2 / width)
    spread = fourier.conj() @ (chirp[:, None] * fourier)
    return block_tables(spread) + block_tables(fourier)


def groups_of(count):
    return [16, count // 16] if count % 16 == 0 and count > 16 else [count]


def split(x):
    high = x.astype(BF16)
    return high, (x - high.astype(F32)).astype(BF16)


def dot(a, b):
    return jnp.dot(a, b, preferred_element_type=F32)


def both_sides(real, imag, right, left_high, left_low):
    width = real.shape[0]
    high, low = split(jnp.concatenate([real, imag], 1))
    mid = dot(jnp.concatenate([high, low, high], 1), right[...])
    high, low = split(jnp.concatenate([mid[:, :width], mid[:, width:]], 0))
    pair = dot(left_high[...], jnp.concatenate([high, low], 1))
    out = pair[:, :width] + pair[:, width:] + dot(left_low[...], high)
    return out[:width], out[width:]


def make_kernel(depth_count, scan_count, slab, width):
    stages = depth_count // 2
    count = 2 * slab
    sides = groups_of(scan_count)
    early = slab

    def kernel(
        row_hbm, col_hbm, objects_hbm, probe_hbm, intensity_hbm, *rest
    ):
        tables_hbm, rest = rest[:6], rest[6:]
        grad, probe_grad, *scratch = rest
        run(row_hbm, col_hbm, objects_hbm, probe_hbm, intensity_hbm, tables_hbm, grad, probe_grad, *scratch)

    def run(
        row_hbm, col_hbm, objects_hbm, probe_hbm, intensity_hbm, tables_hbm, grad, probe_grad,
        right, left_high, left_low, dft_right, dft_left_high, dft_left_low,
        objects, probe, intensity, row_off, col_off, note_out, note_in,
        load_tables, load_objects, load_small, send_note, recv_note,
        sums, store_sums, early_win, far_parts, far_sum, recv_far, send_relay,
        halo_out, pair_out, own_win, halo_win, ext, win, waves, back_in, back, steps, canvas,
        mine, pair_send, pair_in, spill_out, spill_in, seen_out, seen_in, chunks, parts, total, around,
        send_halo, send_pair, send_wave, send_back, send_grad, send_spill, send_seen, send_chunk, send_around,
        recv_halo, recv_pair, recv_wave, recv_back, recv_grad, recv_spill, recv_seen, recv_chunk, recv_around,
    ):
        dep = lax.axis_index("depth")
        me = lax.axis_index("scan")
        stage = dep // 2
        core = dep % 2
        first = stage == 0
        last = stage == stages - 1
        split_core = core == 0
        after = lax.rem(me + 1, scan_count)
        before = lax.rem(me + scan_count - 1, scan_count)
        partner = (dep + 1 - 2 * core, me)
        behind = lax.rem(stage + stages - 1, stages)
        crew = [partner, (2 * behind + core, me)]
        cliques = []
        stride = 1
        for side in sides:
            place = (me // stride) % side
            cliques.append(
                [(dep, me + (lax.rem(place + k, side) - place) * stride) for k in range(1, side)]
            )
            stride *= side
        cliques.reverse()
        friends = crew + [(2 * stage + k, near) for near in (after, before) for k in range(2)]
        for clique in cliques:
            friends = friends + clique

        def copy(source, target, send, recv, device):
            return pltpu.make_async_remote_copy(
                src_ref=source, dst_ref=target, send_sem=send, recv_sem=recv,
                device_id=device, device_id_type=MESH,
            )

        def local(source, target, sem):
            return pltpu.make_async_copy(source, target, sem)

        barrier = pltpu.get_barrier_semaphore()
        for friend in friends:
            pl.semaphore_signal(barrier, inc=1, device_id=friend, device_id_type=MESH)

        loads = [local(row_hbm, row_off, load_small.at[0]), local(col_hbm, col_off, load_small.at[1])]
        object_loads = [local(objects_hbm.at[k], objects.at[k], load_objects.at[k]) for k in range(slab)]
        small_loads = [local(probe_hbm, probe, load_small.at[2]), local(intensity_hbm, intensity, load_small.at[3])]
        tables = [right, left_high, left_low, dft_right, dft_left_high, dft_left_low]
        table_loads = [local(tables_hbm[k], tables[k], load_tables.at[k]) for k in range(6)]
        for load in loads + object_loads + small_loads + table_loads:
            load.start()

        for load in loads:
            load.wait()
        rows_here = [row_off[k] - me * width for k in range(2)]
        second = rows_here[0] != width
        col_split = jnp.where(second, col_off[0], col_off[1])
        col_whole_here = jnp.where(second, col_off[1], col_off[0])
        row_split = jnp.where(second, rows_here[0], rows_here[1])
        rows = jnp.where(split_core, jnp.clip(row_split, 0, width), 0)
        note_out[0] = col_whole_here
        note_out[1] = col_split

        def note_copy():
            return copy(note_out, note_in, send_note, recv_note, (dep, after))

        def halo_copy(k):
            return copy(
                halo_out.at[k], halo_win.at[slab * core + k], send_halo.at[k],
                recv_halo.at[slab * core + k], (2 * stage, before),
            )

        def early_copy(k):
            return copy(
                objects.at[k], early_win.at[k], send_halo.at[k], recv_halo.at[k], (2 * stage, before)
            )

        def pair_copy(k):
            return copy(
                pair_out.at[k], own_win.at[slab * core + k], send_pair.at[k], recv_pair.at[k], partner
            )

        def seen_copy():
            return copy(seen_out, seen_in, send_seen, recv_seen, (dep, after))

        def wave_copy():
            return copy(waves.at[count], waves.at[0], send_wave, recv_wave, (dep + 2, me))

        def back_copy():
            return copy(back, back_in, send_back, recv_back, (dep - 2, me))

        def grad_copy(k):
            return copy(pair_send.at[k], pair_in.at[k], send_grad.at[k], recv_grad.at[k], partner)

        def spill_copy(k):
            return copy(
                spill_out.at[k], spill_in.at[k % slab], send_spill.at[k], recv_spill.at[k % slab],
                (2 * stage + k // slab, after),
            )

        def chunk_copy(target, core_from):
            if False:
                way = 2 if target % 2 == 0 else 7
                return copy(
                    chunks.at[target], far_parts.at[core_from], send_chunk.at[target], recv_far.at[core_from], (way, me)
                )
            return copy(
                chunks.at[target], parts.at[core_from], send_chunk.at[target], recv_chunk.at[core_from], (target, me)
            )

        def relay_copy():
            target = jnp.where(dep == 2, 4, 5)
            return copy(far_sum, parts.at[0], send_relay, recv_chunk.at[0], (target, me))

        def shifted_left(plane, amount):
            return pltpu.roll(plane, lax.rem(2 * width - amount, 2 * width), 1)[:, :width]

        for k in range(slab):
            object_loads[k].wait()
            for part in range(2):
                window = shifted_left(objects[k, part], col_split)

                @pl.when(split_core)
                def _():
                    own_win[k, part] = window

                @pl.when(jnp.logical_not(split_core))
                def _():
                    pair_out[k, part] = window

        pl.semaphore_wait(barrier, len(friends))
        note_copy().start()

        @pl.when(split_core)
        def _():
            for k in range(early):
                early_copy(k).start()

        @pl.when(jnp.logical_not(split_core))
        def _():
            for k in range(slab):
                pair_copy(k).start()

        ext[...] = jnp.zeros_like(ext)
        canvas[...] = jnp.zeros_like(canvas)
        note_copy().wait_recv()
        col_whole = note_in[0]
        col_before = note_in[1]
        col_mine = jnp.where(split_core, col_split, col_whole)
        col_pair = jnp.where(split_core, col_whole, col_split)

        for k in range(slab):
            for part in range(2):
                window = shifted_left(objects[k, part], col_whole)

                @pl.when(split_core)
                def _():
                    pair_out[k, part] = window

                @pl.when(jnp.logical_not(split_core))
                def _():
                    own_win[slab + k, part] = window

            @pl.when(split_core)
            def _():
                pair_copy(k).start()

        for k in range(slab):
            def send_window():
                for part in range(2):
                    halo_out[k, part] = shifted_left(objects[k, part], col_before)
                halo_copy(k).start()

            if k < early:
                pl.when(jnp.logical_not(split_core))(send_window)
            else:
                send_window()

        for load in small_loads + table_loads:
            load.wait()
        measured_split = jnp.where(second, intensity[0], intensity[1])
        measured_whole = jnp.where(second, intensity[1], intensity[0])

        @pl.when(last & (core == 1))
        def _():
            seen_out[...] = measured_whole
            seen_copy().start()

        @pl.when(split_core)
        def _():
            seen_in[...] = measured_split

        def gather_window(k):
            @pl.when(core != k // slab)
            def _():
                copy(
                    pair_out.at[k % slab], own_win.at[k], send_pair.at[k % slab],
                    recv_pair.at[k % slab], partner,
                ).wait_recv()

            @pl.when(split_core)
            def _():
                if k < early:
                    early_copy(k).wait_recv()
                    for part in range(2):
                        ext[part, width:] = shifted_left(early_win[k, part], col_split)
                else:
                    copy(
                        halo_out.at[k % slab], halo_win.at[k], send_halo.at[k % slab],
                        recv_halo.at[k], partner,
                    ).wait_recv()
                    ext[:, width:] = halo_win[k]

            ext[:, :width] = own_win[k]
            for part in range(2):
                win[k, part] = ext[part, pl.ds(rows, width), :]

        def forward(k, real, imag):
            obj_real, obj_imag = win[k, 0], win[k, 1]
            real, imag = both_sides(
                real * obj_real - imag * obj_imag, real * obj_imag + imag * obj_real,
                right, left_high, left_low,
            )
            waves[k + 1, 0] = real
            waves[k + 1, 1] = imag
            return real, imag

        @pl.when(first)
        def _():
            waves[0] = probe[...]
            for k in range(count):
                gather_window(k)
                forward(k, waves[k, 0], waves[k, 1])

        @pl.when(jnp.logical_not(first))
        def _():
            for k in range(count):
                gather_window(k)
            wave_copy().wait_recv()
            real, imag = waves[0, 0], waves[0, 1]
            for k in range(count - 1):
                real, imag = forward(k, real, imag)

            @pl.when(jnp.logical_not(last))
            def _():
                forward(count - 1, real, imag)

        def step_back(k, real, imag):
            wave_real, wave_imag = waves[k, 0], waves[k, 1]
            obj_real, obj_imag = win[k, 0], win[k, 1]
            steps[k, 0] = wave_real * real - wave_imag * imag
            steps[k, 1] = -(wave_real * imag + wave_imag * real)
            return obj_real * real - obj_imag * imag, obj_real * imag + obj_imag * real

        @pl.when(jnp.logical_not(last))
        def _():
            wave_copy().start()
            copy(back, back_in, send_back, recv_back, partner).wait_recv()
            real, imag = both_sides(back_in[0], back_in[1], right, left_high, left_low)
            back[0], back[1] = step_back(count - 1, real, imag)

        @pl.when(last)
        def _():
            pl.when(core == 1)(lambda: seen_copy().wait_recv())
            end = count - 1
            wave_real, wave_imag = waves[end, 0], waves[end, 1]
            obj_real, obj_imag = win[end, 0], win[end, 1]
            real, imag = both_sides(
                wave_real * obj_real - wave_imag * obj_imag, wave_real * obj_imag + wave_imag * obj_real,
                dft_right, dft_left_high, dft_left_low,
            )
            misfit = 2.0 * (real * real + imag * imag - seen_in[...])
            real, imag = both_sides(
                misfit * real, -(misfit * imag), dft_right, dft_left_high, dft_left_low
            )
            back[0], back[1] = step_back(end, real, imag)

        def hand_out(k):
            canvas[:, width:2 * width] = steps[k]
            own = [canvas[part, pl.ds(width - rows, width), :] for part in range(2)]
            at = k % slab

            @pl.when(k // slab == core)
            def _():
                for part in range(2):
                    mine[at, part] = own[part]

            @pl.when(k // slab != core)
            def _():
                for part in range(2):
                    pair_send[at, part] = own[part]
                grad_copy(at).start()

            @pl.when(split_core)
            def _():
                for part in range(2):
                    spill_out[k, part] = canvas[part, pl.ds(2 * width - rows, width), :]
                spill_copy(k).start()

        real, imag = back[0], back[1]
        for k in reversed(range(count - 1)):
            real, imag = both_sides(real, imag, right, left_high, left_low)
            real, imag = step_back(k, real, imag)
            if k == count - 3:
                pl.when(first)(lambda: hand_out(count - 1))
        back[0] = real
        back[1] = imag

        @pl.when(jnp.logical_not(first))
        def _():
            back_copy().start()

        share = width // depth_count

        @pl.when(first)
        def _():
            for k in range(depth_count):
                chunks[k, 0] = back[0, k * share:(k + 1) * share]
                chunks[k, 1] = -back[1, k * share:(k + 1) * share]
            for side in range(2):
                @pl.when(core == side)
                def _():
                    for k in sorted(range(depth_count), key=lambda k: -min(k // 2, stages - k // 2)):
                        if k != side:
                            chunk_copy(k, side).start()
                    parts[side] = chunks[side]

        lax.fori_loop(
            jnp.where(first, 1, 0), count, lambda s, c: (hand_out(count - 1 - s), c)[1], 0
        )

        def await_chunk(k):
            copy(chunks.at[0], parts.at[k], send_chunk.at[0], recv_chunk.at[k], partner).wait_recv()

        if False:
            @pl.when((dep == 2) | (dep == 7))
            def _():
                for k in range(2):
                    copy(chunks.at[0], far_parts.at[k], send_chunk.at[0], recv_far.at[k], partner).wait_recv()
                far_sum[...] = far_parts[0] + far_parts[1]
                relay_copy().start()

        @pl.when(first)
        def _():
            await_chunk(1 - core)

        @pl.when(jnp.logical_not(first))
        def _():
            await_chunk(0)
            await_chunk(1)

        blank = jnp.zeros((width, width), F32)

        def shifted_right(plane, amount):
            return pltpu.roll(jnp.concatenate([plane, blank], 1), amount, 1)

        def add_up(k):
            grad_copy(k).wait_recv()
            copy(spill_out.at[k], spill_in.at[k], send_spill.at[k], recv_spill.at[k], partner).wait_recv()
            for part in range(2):
                grad[k, part] = (
                    shifted_right(mine[k, part], col_mine)
                    + shifted_right(pair_in[k, part], col_pair)
                    + shifted_right(spill_in[k, part], col_before)
                )

        value = parts[0] + parts[1]
        base = 0
        for level, clique in enumerate(cliques):
            total[level] = value
            hops = [
                copy(
                    total.at[level], around.at[base + k], send_around.at[base + k],
                    recv_around.at[base + k], device,
                )
                for k, device in enumerate(clique)
            ]
            for hop in hops:
                hop.start()
            for k in range(slab):
                if (level == 0) == (k > 0) or len(cliques) == 1:
                    add_up(k)
            for k, hop in enumerate(hops):
                hop.wait_recv()
                value = value + around[base + k]
            base += len(clique)
        probe_grad[...] = value

        note_copy().wait_send()
        for k in range(slab):
            if k < early:
                pl.when(split_core)(lambda: early_copy(k).wait_send())
                pl.when(jnp.logical_not(split_core))(lambda: halo_copy(k).wait_send())
            else:
                halo_copy(k).wait_send()
            pair_copy(k).wait_send()
            grad_copy(k).wait_send()

        @pl.when(last & (core == 1))
        def _():
            seen_copy().wait_send()

        @pl.when(split_core)
        def _():
            for k in range(count):
                spill_copy(k).wait_send()

        @pl.when(jnp.logical_not(last))
        def _():
            wave_copy().wait_send()

        @pl.when(jnp.logical_not(first))
        def _():
            back_copy().wait_send()

        @pl.when(first)
        def _():
            for side in range(2):
                @pl.when(core == side)
                def _():
                    for k in range(depth_count):
                        if k != side:
                            chunk_copy(k, side).wait_send()

        if False:
            @pl.when((dep == 2) | (dep == 7))
            def _():
                relay_copy().wait_send()

        base = 0
        for level, clique in enumerate(cliques):
            for k, device in enumerate(clique):
                copy(
                    total.at[level], around.at[base + k], send_around.at[base + k],
                    recv_around.at[base + k], device,
                ).wait_send()
            base += len(clique)

    links = sum(side - 1 for side in sides)
    share = width // depth_count
    plane = (2, width, width)
    buffers = [
        (slab,) + plane, (slab,) + plane, (count,) + plane, (count,) + plane, (2, 2 * width, width),
        (count,) + plane, (count + 1,) + plane, plane, plane, (count,) + plane, (2, 3 * width, width),
        (slab,) + plane, (slab,) + plane, (slab,) + plane, (count,) + plane, (slab,) + plane,
        (width, width), (width, width), (depth_count, 2, share, width), (2, 2, share, width),
        (len(sides), 2, share, width), (links, 2, share, width),
    ]
    dma = pltpu.SemaphoreType.DMA
    marks = [
        dma((slab,)), dma((slab,)), dma, dma, dma((slab,)), dma((count,)), dma, dma((depth_count,)), dma((links,)),
        dma((count,)), dma((slab,)), dma, dma, dma((slab,)), dma((slab,)), dma, dma((2,)), dma((links,)),
    ]
    square = (2 * width, 2 * width)
    tables = [(6 * width, 2 * width), square, square] * 2
    inputs = [(slab, 2, width, 2 * width), plane, plane]
    head = [pltpu.VMEM(shape, BF16) for shape in tables] + [pltpu.VMEM(shape, F32) for shape in inputs]
    head += [pltpu.SMEM((2,), jnp.int32)] * 4
    head += [dma((6,)), dma((slab,)), dma((4,)), dma, dma]
    piece = (2, share, width)
    head += [pltpu.VMEM((slab, 2, width, 2 * width), F32), dma((slab,))]
    head += [pltpu.VMEM((early, 2, width, 2 * width), F32), pltpu.VMEM((2,) + piece, F32), pltpu.VMEM(piece, F32)]
    head += [dma((2,)), dma]
    return kernel, head + [pltpu.VMEM(shape, F32) for shape in buffers] + marks


def body(objects, probe, row_offsets, col_offsets, intensity):
    slab = objects.shape[0]
    width = probe.shape[-1]
    depth_count = lax.axis_size("depth")
    scan_count = lax.axis_size("scan")
    kernel, scratch = make_kernel(depth_count, scan_count, slab, width)
    tables = [jnp.asarray(table) for table in transfer_tables(width)]
    vmem = pl.BlockSpec(memory_space=pltpu.VMEM)
    anywhere = pl.BlockSpec(memory_space=pl.ANY)
    held = pl.pallas_call(
        kernel,
        out_shape=(
            pltpu.VMEM(objects.shape, F32),
            pltpu.VMEM((2, width // depth_count, width), F32),
        ),
        in_specs=[anywhere] * 11,
        out_specs=(vmem, vmem),
        scratch_shapes=scratch,
        compiler_params=pltpu.CompilerParams(
            collective_id=0, has_side_effects=True, vmem_limit_bytes=56 << 20
        ),
        name="slices",
    )(row_offsets, col_offsets, objects, probe, intensity, *tables)

    def store(grad, probe_grad, grad_hbm, probe_grad_hbm, marks):
        moves = [pltpu.make_async_copy(grad.at[k], grad_hbm.at[k], marks.at[k]) for k in range(slab)]
        moves.append(pltpu.make_async_copy(probe_grad, probe_grad_hbm, marks.at[slab]))
        for move in moves:
            move.start()
        for move in moves:
            move.wait()

    return pl.pallas_call(
        store,
        out_shape=tuple(jax.ShapeDtypeStruct(part.shape, F32) for part in held),
        in_specs=[pl.BlockSpec(memory_space=pltpu.VMEM)] * 2,
        compiler_params=pltpu.CompilerParams(vmem_limit_bytes=1 << 20),
        out_specs=(anywhere, anywhere),
        scratch_shapes=[pltpu.SemaphoreType.DMA((slab + 1,))],
        name="store",
    )(*held)


def solution(mesh):
    in_specs = (P("depth", None, "scan", None), P(), P("scan"), P("scan"), P("scan", None, None))
    out_specs = (P("depth", None, "scan", None), P(None, "depth", None))
    return jax.shard_map(body, mesh=mesh, in_specs=in_specs, out_specs=out_specs, check_vma=False)
```

```python
import jax
import jax.numpy as jnp
import ml_dtypes
import numpy as np
from jax import lax
from jax.experimental import pallas as pl
from jax.experimental.pallas import tpu as pltpu
from jax.sharding import PartitionSpec as P

PROPAGATION = 0.5
F32 = jnp.float32
BF16 = jnp.bfloat16
MESH = pl.DeviceIdType.MESH


def split_table(table):
    high = table.astype(ml_dtypes.bfloat16)
    low = (table - high.astype(np.float64)).astype(ml_dtypes.bfloat16)
    return high, low


def block_tables(matrix):
    real, imag = matrix.real, matrix.imag
    right_high, right_low = split_table(np.block([[real, imag], [-imag, real]]))
    left_high, left_low = split_table(np.block([[real, -imag], [imag, real]]))
    return np.concatenate([right_high, right_high, right_low], 0), left_high, left_low


def transfer_tables(width):
    index = np.arange(width)
    frequency = np.where(index < width // 2, index, index - width).astype(np.float64)
    fourier = np.exp(-2j * np.pi * (np.outer(index, index) % width) / width) / np.sqrt(width)
    chirp = np.exp(-1j * PROPAGATION * np.pi * frequency**2 / width)
    spread = fourier.conj() @ (chirp[:, None] * fourier)
    return block_tables(spread) + block_tables(fourier)


def groups_of(count):
    return [16, count // 16] if count % 16 == 0 and count > 16 else [count]


def split(x):
    high = x.astype(BF16)
    return high, (x - high.astype(F32)).astype(BF16)


def dot(a, b):
    return jnp.dot(a, b, preferred_element_type=F32)


def both_sides(real, imag, right, left_high, left_low):
    width = real.shape[0]
    high, low = split(jnp.concatenate([real, imag], 1))
    mid = dot(jnp.concatenate([high, low, high], 1), right[...])
    high, low = split(jnp.concatenate([mid[:, :width], mid[:, width:]], 0))
    pair = dot(left_high[...], jnp.concatenate([high, low], 1))
    out = pair[:, :width] + pair[:, width:] + dot(left_low[...], high)
    return out[:width], out[width:]


def make_kernel(depth_count, scan_count, slab, width):
    stages = depth_count // 2
    count = 2 * slab
    sides = groups_of(scan_count)
    early = slab

    def kernel(
        row_hbm, col_hbm, objects_hbm, probe_hbm, intensity_hbm, *rest
    ):
        tables_hbm, rest = rest[:6], rest[6:]
        grad, probe_grad, *scratch = rest
        run(row_hbm, col_hbm, objects_hbm, probe_hbm, intensity_hbm, tables_hbm, grad, probe_grad, *scratch)

    def run(
        row_hbm, col_hbm, objects_hbm, probe_hbm, intensity_hbm, tables_hbm, grad, probe_grad,
        right, left_high, left_low, dft_right, dft_left_high, dft_left_low,
        objects, probe, intensity, row_off, col_off, note_out, note_in,
        load_tables, load_objects, load_small, send_note, recv_note,
        sums, store_sums, early_win, far_parts, far_sum, recv_far, send_relay,
        halo_out, pair_out, own_win, halo_win, ext, win, waves, back_in, back, steps, canvas,
        mine, pair_send, pair_in, spill_out, spill_in, seen_out, seen_in, chunks, parts, total, around,
        send_halo, send_pair, send_wave, send_back, send_grad, send_spill, send_seen, send_chunk, send_around,
        recv_halo, recv_pair, recv_wave, recv_back, recv_grad, recv_spill, recv_seen, recv_chunk, recv_around,
    ):
        dep = lax.axis_index("depth")
        me = lax.axis_index("scan")
        stage = dep // 2
        core = dep % 2
        first = stage == 0
        last = stage == stages - 1
        split_core = core == 0
        after = lax.rem(me + 1, scan_count)
        before = lax.rem(me + scan_count - 1, scan_count)
        partner = (dep + 1 - 2 * core, me)
        behind = lax.rem(stage + stages - 1, stages)
        crew = [partner, (2 * behind + core, me)]
        cliques = []
        stride = 1
        for side in sides:
            place = (me // stride) % side
            if side == 16:
                across, along = place % 4, place // 4
                moves = [(k % 4, k // 4) for k in range(1, 16)]
                moves.sort(key=lambda move: -min(move[0], 4 - move[0]) - min(move[1], 4 - move[1]))
                peers = [lax.rem(along + q, 4) * 4 + lax.rem(across + p, 4) for p, q in moves]
            else:
                peers = [lax.rem(place + k, side) for k in range(1, side)]
            cliques.append([(dep, me + (peer - place) * stride) for peer in peers])
            stride *= side
        cliques.reverse()
        friends = crew + [(2 * stage + k, near) for near in (after, before) for k in range(2)]
        for clique in cliques:
            friends = friends + clique

        def copy(source, target, send, recv, device):
            return pltpu.make_async_remote_copy(
                src_ref=source, dst_ref=target, send_sem=send, recv_sem=recv,
                device_id=device, device_id_type=MESH,
            )

        def local(source, target, sem):
            return pltpu.make_async_copy(source, target, sem)

        barrier = pltpu.get_barrier_semaphore()
        for friend in friends:
            pl.semaphore_signal(barrier, inc=1, device_id=friend, device_id_type=MESH)

        loads = [local(row_hbm, row_off, load_small.at[0]), local(col_hbm, col_off, load_small.at[1])]
        object_loads = [local(objects_hbm.at[k], objects.at[k], load_objects.at[k]) for k in range(slab)]
        small_loads = [local(probe_hbm, probe, load_small.at[2]), local(intensity_hbm, intensity, load_small.at[3])]
        tables = [right, left_high, left_low, dft_right, dft_left_high, dft_left_low]
        table_loads = [local(tables_hbm[k], tables[k], load_tables.at[k]) for k in range(6)]
        for load in loads + object_loads + small_loads + table_loads:
            load.start()

        for load in loads:
            load.wait()
        rows_here = [row_off[k] - me * width for k in range(2)]
        second = rows_here[0] != width
        col_split = jnp.where(second, col_off[0], col_off[1])
        col_whole_here = jnp.where(second, col_off[1], col_off[0])
        row_split = jnp.where(second, rows_here[0], rows_here[1])
        rows = jnp.where(split_core, jnp.clip(row_split, 0, width), 0)
        note_out[0] = col_whole_here
        note_out[1] = col_split

        def note_copy():
            return copy(note_out, note_in, send_note, recv_note, (dep, after))

        def halo_copy(k):
            return copy(
                halo_out.at[k], halo_win.at[slab * core + k], send_halo.at[k],
                recv_halo.at[slab * core + k], (2 * stage, before),
            )

        def early_copy(k):
            return copy(
                objects.at[k], early_win.at[k], send_halo.at[k], recv_halo.at[k], (2 * stage, before)
            )

        def pair_copy(k):
            return copy(
                pair_out.at[k], own_win.at[slab * core + k], send_pair.at[k], recv_pair.at[k], partner
            )

        def seen_copy():
            return copy(seen_out, seen_in, send_seen, recv_seen, (dep, after))

        def wave_copy():
            return copy(waves.at[count], waves.at[0], send_wave, recv_wave, (dep + 2, me))

        def back_copy():
            return copy(back, back_in, send_back, recv_back, (dep - 2, me))

        def grad_copy(k):
            return copy(pair_send.at[k], pair_in.at[k], send_grad.at[k], recv_grad.at[k], partner)

        def spill_copy(k):
            return copy(
                spill_out.at[k], spill_in.at[k % slab], send_spill.at[k], recv_spill.at[k % slab],
                (2 * stage + k // slab, after),
            )

        def chunk_copy(target, core_from):
            if False:
                way = 2 if target % 2 == 0 else 7
                return copy(
                    chunks.at[target], far_parts.at[core_from], send_chunk.at[target], recv_far.at[core_from], (way, me)
                )
            return copy(
                chunks.at[target], parts.at[core_from], send_chunk.at[target], recv_chunk.at[core_from], (target, me)
            )

        def relay_copy():
            target = jnp.where(dep == 2, 4, 5)
            return copy(far_sum, parts.at[0], send_relay, recv_chunk.at[0], (target, me))

        def shifted_left(plane, amount):
            return pltpu.roll(plane, lax.rem(2 * width - amount, 2 * width), 1)[:, :width]

        for k in range(slab):
            object_loads[k].wait()
            for part in range(2):
                window = shifted_left(objects[k, part], col_split)

                @pl.when(split_core)
                def _():
                    own_win[k, part] = window

                @pl.when(jnp.logical_not(split_core))
                def _():
                    pair_out[k, part] = window

        pl.semaphore_wait(barrier, len(friends))
        note_copy().start()

        @pl.when(split_core)
        def _():
            for k in range(early):
                early_copy(k).start()

        @pl.when(jnp.logical_not(split_core))
        def _():
            for k in range(slab):
                pair_copy(k).start()

        ext[...] = jnp.zeros_like(ext)
        canvas[...] = jnp.zeros_like(canvas)
        note_copy().wait_recv()
        col_whole = note_in[0]
        col_before = note_in[1]
        col_mine = jnp.where(split_core, col_split, col_whole)
        col_pair = jnp.where(split_core, col_whole, col_split)

        for k in range(slab):
            for part in range(2):
                window = shifted_left(objects[k, part], col_whole)

                @pl.when(split_core)
                def _():
                    pair_out[k, part] = window

                @pl.when(jnp.logical_not(split_core))
                def _():
                    own_win[slab + k, part] = window

            @pl.when(split_core)
            def _():
                pair_copy(k).start()

        for k in range(slab):
            def send_window():
                for part in range(2):
                    halo_out[k, part] = shifted_left(objects[k, part], col_before)
                halo_copy(k).start()

            if k < early:
                pl.when(jnp.logical_not(split_core))(send_window)
            else:
                send_window()

        for load in small_loads + table_loads:
            load.wait()
        measured_split = jnp.where(second, intensity[0], intensity[1])
        measured_whole = jnp.where(second, intensity[1], intensity[0])

        @pl.when(last & (core == 1))
        def _():
            seen_out[...] = measured_whole
            seen_copy().start()

        @pl.when(split_core)
        def _():
            seen_in[...] = measured_split

        def gather_window(k):
            @pl.when(core != k // slab)
            def _():
                copy(
                    pair_out.at[k % slab], own_win.at[k], send_pair.at[k % slab],
                    recv_pair.at[k % slab], partner,
                ).wait_recv()

            @pl.when(split_core)
            def _():
                if k < early:
                    early_copy(k).wait_recv()
                    for part in range(2):
                        ext[part, width:] = shifted_left(early_win[k, part], col_split)
                else:
                    copy(
                        halo_out.at[k % slab], halo_win.at[k], send_halo.at[k % slab],
                        recv_halo.at[k], partner,
                    ).wait_recv()
                    ext[:, width:] = halo_win[k]

            ext[:, :width] = own_win[k]
            for part in range(2):
                win[k, part] = ext[part, pl.ds(rows, width), :]

        def forward(k, real, imag):
            obj_real, obj_imag = win[k, 0], win[k, 1]
            real, imag = both_sides(
                real * obj_real - imag * obj_imag, real * obj_imag + imag * obj_real,
                right, left_high, left_low,
            )
            waves[k + 1, 0] = real
            waves[k + 1, 1] = imag
            return real, imag

        @pl.when(first)
        def _():
            waves[0] = probe[...]
            for k in range(count):
                gather_window(k)
                forward(k, waves[k, 0], waves[k, 1])

        @pl.when(jnp.logical_not(first))
        def _():
            for k in range(count):
                gather_window(k)
            wave_copy().wait_recv()
            real, imag = waves[0, 0], waves[0, 1]
            for k in range(count - 1):
                real, imag = forward(k, real, imag)

            @pl.when(jnp.logical_not(last))
            def _():
                forward(count - 1, real, imag)

        def step_back(k, real, imag):
            wave_real, wave_imag = waves[k, 0], waves[k, 1]
            obj_real, obj_imag = win[k, 0], win[k, 1]
            steps[k, 0] = wave_real * real - wave_imag * imag
            steps[k, 1] = -(wave_real * imag + wave_imag * real)
            return obj_real * real - obj_imag * imag, obj_real * imag + obj_imag * real

        @pl.when(jnp.logical_not(last))
        def _():
            wave_copy().start()
            copy(back, back_in, send_back, recv_back, partner).wait_recv()
            real, imag = both_sides(back_in[0], back_in[1], right, left_high, left_low)
            back[0], back[1] = step_back(count - 1, real, imag)

        @pl.when(last)
        def _():
            pl.when(core == 1)(lambda: seen_copy().wait_recv())
            end = count - 1
            wave_real, wave_imag = waves[end, 0], waves[end, 1]
            obj_real, obj_imag = win[end, 0], win[end, 1]
            real, imag = both_sides(
                wave_real * obj_real - wave_imag * obj_imag, wave_real * obj_imag + wave_imag * obj_real,
                dft_right, dft_left_high, dft_left_low,
            )
            misfit = 2.0 * (real * real + imag * imag - seen_in[...])
            real, imag = both_sides(
                misfit * real, -(misfit * imag), dft_right, dft_left_high, dft_left_low
            )
            back[0], back[1] = step_back(end, real, imag)

        def hand_out(k):
            canvas[:, width:2 * width] = steps[k]
            own = [canvas[part, pl.ds(width - rows, width), :] for part in range(2)]
            at = k % slab

            @pl.when(k // slab == core)
            def _():
                for part in range(2):
                    mine[at, part] = own[part]

            @pl.when(k // slab != core)
            def _():
                for part in range(2):
                    pair_send[at, part] = own[part]
                grad_copy(at).start()

            @pl.when(split_core)
            def _():
                for part in range(2):
                    spill_out[k, part] = canvas[part, pl.ds(2 * width - rows, width), :]
                spill_copy(k).start()

        real, imag = back[0], back[1]
        for k in reversed(range(count - 1)):
            real, imag = both_sides(real, imag, right, left_high, left_low)
            real, imag = step_back(k, real, imag)
            if k == count - 3:
                pl.when(first)(lambda: hand_out(count - 1))
        back[0] = real
        back[1] = imag

        @pl.when(jnp.logical_not(first))
        def _():
            back_copy().start()

        share = width // depth_count

        @pl.when(first)
        def _():
            for k in range(depth_count):
                chunks[k, 0] = back[0, k * share:(k + 1) * share]
                chunks[k, 1] = -back[1, k * share:(k + 1) * share]
            for side in range(2):
                @pl.when(core == side)
                def _():
                    for k in sorted(range(depth_count), key=lambda k: -min(k // 2, stages - k // 2)):
                        if k != side:
                            chunk_copy(k, side).start()
                    parts[side] = chunks[side]

        lax.fori_loop(
            jnp.where(first, 1, 0), count, lambda s, c: (hand_out(count - 1 - s), c)[1], 0
        )

        def await_chunk(k):
            copy(chunks.at[0], parts.at[k], send_chunk.at[0], recv_chunk.at[k], partner).wait_recv()

        if False:
            @pl.when((dep == 2) | (dep == 7))
            def _():
                for k in range(2):
                    copy(chunks.at[0], far_parts.at[k], send_chunk.at[0], recv_far.at[k], partner).wait_recv()
                far_sum[...] = far_parts[0] + far_parts[1]
                relay_copy().start()

        @pl.when(first)
        def _():
            await_chunk(1 - core)

        @pl.when(jnp.logical_not(first))
        def _():
            await_chunk(0)
            await_chunk(1)

        blank = jnp.zeros((width, width), F32)

        def shifted_right(plane, amount):
            return pltpu.roll(jnp.concatenate([plane, blank], 1), amount, 1)

        def add_up(k):
            grad_copy(k).wait_recv()
            copy(spill_out.at[k], spill_in.at[k], send_spill.at[k], recv_spill.at[k], partner).wait_recv()
            for part in range(2):
                grad[k, part] = (
                    shifted_right(mine[k, part], col_mine)
                    + shifted_right(pair_in[k, part], col_pair)
                    + shifted_right(spill_in[k, part], col_before)
                )

        value = parts[0] + parts[1]
        base = 0
        for level, clique in enumerate(cliques):
            total[level] = value
            hops = [
                copy(
                    total.at[level], around.at[base + k], send_around.at[base + k],
                    recv_around.at[base + k], device,
                )
                for k, device in enumerate(clique)
            ]
            for hop in hops:
                hop.start()
            for k in range(slab):
                if level == len(cliques) - 1:
                    add_up(k)
            for k, hop in enumerate(hops):
                hop.wait_recv()
                value = value + around[base + k]
            base += len(clique)
        probe_grad[...] = value

        note_copy().wait_send()
        for k in range(slab):
            if k < early:
                pl.when(split_core)(lambda: early_copy(k).wait_send())
                pl.when(jnp.logical_not(split_core))(lambda: halo_copy(k).wait_send())
            else:
                halo_copy(k).wait_send()
            pair_copy(k).wait_send()
            grad_copy(k).wait_send()

        @pl.when(last & (core == 1))
        def _():
            seen_copy().wait_send()

        @pl.when(split_core)
        def _():
            for k in range(count):
                spill_copy(k).wait_send()

        @pl.when(jnp.logical_not(last))
        def _():
            wave_copy().wait_send()

        @pl.when(jnp.logical_not(first))
        def _():
            back_copy().wait_send()

        @pl.when(first)
        def _():
            for side in range(2):
                @pl.when(core == side)
                def _():
                    for k in range(depth_count):
                        if k != side:
                            chunk_copy(k, side).wait_send()

        if False:
            @pl.when((dep == 2) | (dep == 7))
            def _():
                relay_copy().wait_send()

        base = 0
        for level, clique in enumerate(cliques):
            for k, device in enumerate(clique):
                copy(
                    total.at[level], around.at[base + k], send_around.at[base + k],
                    recv_around.at[base + k], device,
                ).wait_send()
            base += len(clique)

    links = sum(side - 1 for side in sides)
    share = width // depth_count
    plane = (2, width, width)
    buffers = [
        (slab,) + plane, (slab,) + plane, (count,) + plane, (count,) + plane, (2, 2 * width, width),
        (count,) + plane, (count + 1,) + plane, plane, plane, (count,) + plane, (2, 3 * width, width),
        (slab,) + plane, (slab,) + plane, (slab,) + plane, (count,) + plane, (slab,) + plane,
        (width, width), (width, width), (depth_count, 2, share, width), (2, 2, share, width),
        (len(sides), 2, share, width), (links, 2, share, width),
    ]
    dma = pltpu.SemaphoreType.DMA
    marks = [
        dma((slab,)), dma((slab,)), dma, dma, dma((slab,)), dma((count,)), dma, dma((depth_count,)), dma((links,)),
        dma((count,)), dma((slab,)), dma, dma, dma((slab,)), dma((slab,)), dma, dma((2,)), dma((links,)),
    ]
    square = (2 * width, 2 * width)
    tables = [(6 * width, 2 * width), square, square] * 2
    inputs = [(slab, 2, width, 2 * width), plane, plane]
    head = [pltpu.VMEM(shape, BF16) for shape in tables] + [pltpu.VMEM(shape, F32) for shape in inputs]
    head += [pltpu.SMEM((2,), jnp.int32)] * 4
    head += [dma((6,)), dma((slab,)), dma((4,)), dma, dma]
    piece = (2, share, width)
    head += [pltpu.VMEM((slab, 2, width, 2 * width), F32), dma((slab,))]
    head += [pltpu.VMEM((early, 2, width, 2 * width), F32), pltpu.VMEM((2,) + piece, F32), pltpu.VMEM(piece, F32)]
    head += [dma((2,)), dma]
    return kernel, head + [pltpu.VMEM(shape, F32) for shape in buffers] + marks


def body(objects, probe, row_offsets, col_offsets, intensity):
    slab = objects.shape[0]
    width = probe.shape[-1]
    depth_count = lax.axis_size("depth")
    scan_count = lax.axis_size("scan")
    kernel, scratch = make_kernel(depth_count, scan_count, slab, width)
    tables = [jnp.asarray(table) for table in transfer_tables(width)]
    vmem = pl.BlockSpec(memory_space=pltpu.VMEM)
    anywhere = pl.BlockSpec(memory_space=pl.ANY)
    held = pl.pallas_call(
        kernel,
        out_shape=(
            pltpu.VMEM(objects.shape, F32),
            pltpu.VMEM((2, width // depth_count, width), F32),
        ),
        in_specs=[anywhere] * 11,
        out_specs=(vmem, vmem),
        scratch_shapes=scratch,
        compiler_params=pltpu.CompilerParams(
            collective_id=0, has_side_effects=True, vmem_limit_bytes=56 << 20
        ),
        name="slices",
    )(row_offsets, col_offsets, objects, probe, intensity, *tables)

    def store(grad, probe_grad, grad_hbm, probe_grad_hbm, marks):
        moves = [pltpu.make_async_copy(grad.at[k], grad_hbm.at[k], marks.at[k]) for k in range(slab)]
        moves.append(pltpu.make_async_copy(probe_grad, probe_grad_hbm, marks.at[slab]))
        for move in moves:
            move.start()
        for move in moves:
            move.wait()

    return pl.pallas_call(
        store,
        out_shape=tuple(jax.ShapeDtypeStruct(part.shape, F32) for part in held),
        in_specs=[pl.BlockSpec(memory_space=pltpu.VMEM)] * 2,
        compiler_params=pltpu.CompilerParams(vmem_limit_bytes=1 << 20),
        out_specs=(anywhere, anywhere),
        scratch_shapes=[pltpu.SemaphoreType.DMA((slab + 1,))],
        name="store",
    )(*held)


def solution(mesh):
    in_specs = (P("depth", None, "scan", None), P(), P("scan"), P("scan"), P("scan", None, None))
    out_specs = (P("depth", None, "scan", None), P(None, "depth", None))
    return jax.shard_map(body, mesh=mesh, in_specs=in_specs, out_specs=out_specs, check_vma=False)
```

```python
import jax
import jax.numpy as jnp
import ml_dtypes
import numpy as np
from jax import lax
from jax.experimental import pallas as pl
from jax.experimental.pallas import tpu as pltpu
from jax.sharding import PartitionSpec as P

PROPAGATION = 0.5
F32 = jnp.float32
BF16 = jnp.bfloat16
MESH = pl.DeviceIdType.MESH


def split_table(table):
    high = table.astype(ml_dtypes.bfloat16)
    low = (table - high.astype(np.float64)).astype(ml_dtypes.bfloat16)
    return high, low


def block_tables(matrix):
    real, imag = matrix.real, matrix.imag
    right_high, right_low = split_table(np.block([[real, imag], [-imag, real]]))
    left_high, left_low = split_table(np.block([[real, -imag], [imag, real]]))
    return np.concatenate([right_high, right_high, right_low], 0), left_high, left_low


def transfer_tables(width):
    index = np.arange(width)
    frequency = np.where(index < width // 2, index, index - width).astype(np.float64)
    fourier = np.exp(-2j * np.pi * (np.outer(index, index) % width) / width) / np.sqrt(width)
    chirp = np.exp(-1j * PROPAGATION * np.pi * frequency**2 / width)
    spread = fourier.conj() @ (chirp[:, None] * fourier)
    return block_tables(spread) + block_tables(fourier)


def groups_of(count):
    return [16, count // 16] if count % 16 == 0 and count > 16 else [count]


def split(x):
    high = x.astype(BF16)
    return high, (x - high.astype(F32)).astype(BF16)


def dot(a, b):
    return jnp.dot(a, b, preferred_element_type=F32)


def both_sides(real, imag, right, left_high, left_low):
    width = real.shape[0]
    high, low = split(jnp.concatenate([real, imag], 1))
    mid = dot(jnp.concatenate([high, low, high], 1), right[...])
    high, low = split(jnp.concatenate([mid[:, :width], mid[:, width:]], 0))
    pair = dot(left_high[...], jnp.concatenate([high, low], 1))
    out = pair[:, :width] + pair[:, width:] + dot(left_low[...], high)
    return out[:width], out[width:]


def make_kernel(depth_count, scan_count, slab, width):
    stages = depth_count // 2
    count = 2 * slab
    sides = groups_of(scan_count)
    early = slab

    def kernel(
        row_hbm, col_hbm, objects_hbm, probe_hbm, intensity_hbm, *rest
    ):
        tables_hbm, rest = rest[:6], rest[6:]
        grad, probe_grad, *scratch = rest
        run(row_hbm, col_hbm, objects_hbm, probe_hbm, intensity_hbm, tables_hbm, grad, probe_grad, *scratch)

    def run(
        row_hbm, col_hbm, objects_hbm, probe_hbm, intensity_hbm, tables_hbm, grad, probe_grad,
        right, left_high, left_low, dft_right, dft_left_high, dft_left_low,
        objects, probe, intensity, row_off, col_off, note_out, note_in,
        load_tables, load_objects, load_small, send_note, recv_note,
        sums, store_sums, early_win, far_parts, far_sum, recv_far, send_relay,
        halo_out, pair_out, own_win, halo_win, ext, win, waves, back_in, back, steps, canvas,
        mine, pair_send, pair_in, spill_out, spill_in, seen_out, seen_in, chunks, parts, total, around,
        send_halo, send_pair, send_wave, send_back, send_grad, send_spill, send_seen, send_chunk, send_around,
        recv_halo, recv_pair, recv_wave, recv_back, recv_grad, recv_spill, recv_seen, recv_chunk, recv_around,
    ):
        dep = lax.axis_index("depth")
        me = lax.axis_index("scan")
        stage = dep // 2
        core = dep % 2
        first = stage == 0
        last = stage == stages - 1
        split_core = core == 0
        after = lax.rem(me + 1, scan_count)
        before = lax.rem(me + scan_count - 1, scan_count)
        partner = (dep + 1 - 2 * core, me)
        behind = lax.rem(stage + stages - 1, stages)
        crew = [partner, (2 * behind + core, me)]
        cliques = []
        stride = 1
        for side in sides:
            place = (me // stride) % side
            if side == 16:
                across, along = place % 4, place // 4
                moves = [(k % 4, k // 4) for k in range(1, 16)]
                moves.sort(key=lambda move: -min(move[0], 4 - move[0]) - min(move[1], 4 - move[1]))
                peers = [lax.rem(along + q, 4) * 4 + lax.rem(across + p, 4) for p, q in moves]
            else:
                peers = [lax.rem(place + k, side) for k in range(1, side)]
            cliques.append([(dep, me + (peer - place) * stride) for peer in peers])
            stride *= side
        cliques.reverse()
        friends = crew + [(dep, before)]
        for clique in cliques:
            friends = friends + clique

        def copy(source, target, send, recv, device):
            return pltpu.make_async_remote_copy(
                src_ref=source, dst_ref=target, send_sem=send, recv_sem=recv,
                device_id=device, device_id_type=MESH,
            )

        def local(source, target, sem):
            return pltpu.make_async_copy(source, target, sem)

        barrier = pltpu.get_barrier_semaphore()
        for friend in friends:
            pl.semaphore_signal(barrier, inc=1, device_id=friend, device_id_type=MESH)

        @pl.when(core == 0)
        def _():
            for k in range(2):
                pl.semaphore_signal(barrier, inc=1, device_id=(2 * stage + k, after), device_id_type=MESH)

        loads = [local(row_hbm, row_off, load_small.at[0]), local(col_hbm, col_off, load_small.at[1])]
        object_loads = [local(objects_hbm.at[k], objects.at[k], load_objects.at[k]) for k in range(slab)]
        small_loads = [local(probe_hbm, probe, load_small.at[2]), local(intensity_hbm, intensity, load_small.at[3])]
        tables = [right, left_high, left_low, dft_right, dft_left_high, dft_left_low]
        table_loads = [local(tables_hbm[k], tables[k], load_tables.at[k]) for k in range(6)]
        for load in loads + object_loads + small_loads + table_loads:
            load.start()

        for load in loads:
            load.wait()
        rows_here = [row_off[k] - me * width for k in range(2)]
        second = rows_here[0] != width
        col_split = jnp.where(second, col_off[0], col_off[1])
        col_whole_here = jnp.where(second, col_off[1], col_off[0])
        row_split = jnp.where(second, rows_here[0], rows_here[1])
        rows = jnp.where(split_core, jnp.clip(row_split, 0, width), 0)
        note_out[0] = col_whole_here
        note_out[1] = col_split

        def note_copy():
            return copy(note_out, note_in, send_note, recv_note, (dep, after))

        def halo_copy(k):
            return copy(
                halo_out.at[k], halo_win.at[slab * core + k], send_halo.at[k],
                recv_halo.at[slab * core + k], (2 * stage, before),
            )

        def early_copy(k):
            return copy(
                objects.at[k], early_win.at[k], send_halo.at[k], recv_halo.at[k], (2 * stage, before)
            )

        def pair_copy(k):
            return copy(
                pair_out.at[k], own_win.at[slab * core + k], send_pair.at[k], recv_pair.at[k], partner
            )

        def seen_copy():
            return copy(seen_out, seen_in, send_seen, recv_seen, (dep, after))

        def wave_copy():
            return copy(waves.at[count], waves.at[0], send_wave, recv_wave, (dep + 2, me))

        def back_copy():
            return copy(back, back_in, send_back, recv_back, (dep - 2, me))

        def grad_copy(k):
            return copy(pair_send.at[k], pair_in.at[k], send_grad.at[k], recv_grad.at[k], partner)

        def spill_copy(k):
            return copy(
                spill_out.at[k], spill_in.at[k % slab], send_spill.at[k], recv_spill.at[k % slab],
                (2 * stage + k // slab, after),
            )

        def chunk_copy(target, core_from):
            if False:
                way = 2 if target % 2 == 0 else 7
                return copy(
                    chunks.at[target], far_parts.at[core_from], send_chunk.at[target], recv_far.at[core_from], (way, me)
                )
            return copy(
                chunks.at[target], parts.at[core_from], send_chunk.at[target], recv_chunk.at[core_from], (target, me)
            )

        def relay_copy():
            target = jnp.where(dep == 2, 4, 5)
            return copy(far_sum, parts.at[0], send_relay, recv_chunk.at[0], (target, me))

        def shifted_left(plane, amount):
            return pltpu.roll(plane, lax.rem(2 * width - amount, 2 * width), 1)[:, :width]

        for k in range(slab):
            object_loads[k].wait()
            for part in range(2):
                window = shifted_left(objects[k, part], col_split)

                @pl.when(split_core)
                def _():
                    own_win[k, part] = window

                @pl.when(jnp.logical_not(split_core))
                def _():
                    pair_out[k, part] = window

        pl.semaphore_wait(barrier, len(friends) + 1)
        note_copy().start()

        @pl.when(split_core)
        def _():
            for k in range(early):
                early_copy(k).start()

        @pl.when(jnp.logical_not(split_core))
        def _():
            for k in range(slab):
                pair_copy(k).start()

        ext[...] = jnp.zeros_like(ext)
        canvas[...] = jnp.zeros_like(canvas)
        note_copy().wait_recv()
        col_whole = note_in[0]
        col_before = note_in[1]
        col_mine = jnp.where(split_core, col_split, col_whole)
        col_pair = jnp.where(split_core, col_whole, col_split)

        for k in range(slab):
            for part in range(2):
                window = shifted_left(objects[k, part], col_whole)

                @pl.when(split_core)
                def _():
                    pair_out[k, part] = window

                @pl.when(jnp.logical_not(split_core))
                def _():
                    own_win[slab + k, part] = window

            @pl.when(split_core)
            def _():
                pair_copy(k).start()

        for k in range(slab):
            def send_window():
                for part in range(2):
                    halo_out[k, part] = shifted_left(objects[k, part], col_before)
                halo_copy(k).start()

            if k < early:
                pl.when(jnp.logical_not(split_core))(send_window)
            else:
                send_window()

        for load in small_loads + table_loads:
            load.wait()
        measured_split = jnp.where(second, intensity[0], intensity[1])
        measured_whole = jnp.where(second, intensity[1], intensity[0])

        @pl.when(last & (core == 1))
        def _():
            seen_out[...] = measured_whole
            seen_copy().start()

        @pl.when(split_core)
        def _():
            seen_in[...] = measured_split

        def gather_window(k):
            @pl.when(core != k // slab)
            def _():
                copy(
                    pair_out.at[k % slab], own_win.at[k], send_pair.at[k % slab],
                    recv_pair.at[k % slab], partner,
                ).wait_recv()

            @pl.when(split_core)
            def _():
                if k < early:
                    early_copy(k).wait_recv()
                    for part in range(2):
                        ext[part, width:] = shifted_left(early_win[k, part], col_split)
                else:
                    copy(
                        halo_out.at[k % slab], halo_win.at[k], send_halo.at[k % slab],
                        recv_halo.at[k], partner,
                    ).wait_recv()
                    ext[:, width:] = halo_win[k]

            ext[:, :width] = own_win[k]
            for part in range(2):
                win[k, part] = ext[part, pl.ds(rows, width), :]

        def forward(k, real, imag):
            obj_real, obj_imag = win[k, 0], win[k, 1]
            real, imag = both_sides(
                real * obj_real - imag * obj_imag, real * obj_imag + imag * obj_real,
                right, left_high, left_low,
            )
            waves[k + 1, 0] = real
            waves[k + 1, 1] = imag
            return real, imag

        @pl.when(first)
        def _():
            waves[0] = probe[...]
            for k in range(count):
                gather_window(k)
                forward(k, waves[k, 0], waves[k, 1])

        @pl.when(jnp.logical_not(first))
        def _():
            for k in range(count):
                gather_window(k)
            wave_copy().wait_recv()
            real, imag = waves[0, 0], waves[0, 1]
            for k in range(count - 1):
                real, imag = forward(k, real, imag)

            @pl.when(jnp.logical_not(last))
            def _():
                forward(count - 1, real, imag)

        def step_back(k, real, imag):
            wave_real, wave_imag = waves[k, 0], waves[k, 1]
            obj_real, obj_imag = win[k, 0], win[k, 1]
            steps[k, 0] = wave_real * real - wave_imag * imag
            steps[k, 1] = -(wave_real * imag + wave_imag * real)
            return obj_real * real - obj_imag * imag, obj_real * imag + obj_imag * real

        @pl.when(jnp.logical_not(last))
        def _():
            wave_copy().start()
            copy(back, back_in, send_back, recv_back, partner).wait_recv()
            real, imag = both_sides(back_in[0], back_in[1], right, left_high, left_low)
            back[0], back[1] = step_back(count - 1, real, imag)

        @pl.when(last)
        def _():
            pl.when(core == 1)(lambda: seen_copy().wait_recv())
            end = count - 1
            wave_real, wave_imag = waves[end, 0], waves[end, 1]
            obj_real, obj_imag = win[end, 0], win[end, 1]
            real, imag = both_sides(
                wave_real * obj_real - wave_imag * obj_imag, wave_real * obj_imag + wave_imag * obj_real,
                dft_right, dft_left_high, dft_left_low,
            )
            misfit = 2.0 * (real * real + imag * imag - seen_in[...])
            real, imag = both_sides(
                misfit * real, -(misfit * imag), dft_right, dft_left_high, dft_left_low
            )
            back[0], back[1] = step_back(end, real, imag)

        def hand_out(k):
            canvas[:, width:2 * width] = steps[k]
            own = [canvas[part, pl.ds(width - rows, width), :] for part in range(2)]
            at = k % slab

            @pl.when(k // slab == core)
            def _():
                for part in range(2):
                    mine[at, part] = own[part]

            @pl.when(k // slab != core)
            def _():
                for part in range(2):
                    pair_send[at, part] = own[part]
                grad_copy(at).start()

            @pl.when(split_core)
            def _():
                for part in range(2):
                    spill_out[k, part] = canvas[part, pl.ds(2 * width - rows, width), :]
                spill_copy(k).start()

        real, imag = back[0], back[1]
        for k in reversed(range(count - 1)):
            real, imag = both_sides(real, imag, right, left_high, left_low)
            real, imag = step_back(k, real, imag)
            if k == count - 3:
                pl.when(first)(lambda: hand_out(count - 1))
        back[0] = real
        back[1] = imag

        @pl.when(jnp.logical_not(first))
        def _():
            back_copy().start()

        share = width // depth_count

        @pl.when(first)
        def _():
            for k in range(depth_count):
                chunks[k, 0] = back[0, k * share:(k + 1) * share]
                chunks[k, 1] = -back[1, k * share:(k + 1) * share]
            for side in range(2):
                @pl.when(core == side)
                def _():
                    for k in sorted(range(depth_count), key=lambda k: -min(k // 2, stages - k // 2)):
                        if k != side:
                            chunk_copy(k, side).start()
                    parts[side] = chunks[side]

        lax.fori_loop(
            jnp.where(first, 1, 0), count, lambda s, c: (hand_out(count - 1 - s), c)[1], 0
        )

        def await_chunk(k):
            copy(chunks.at[0], parts.at[k], send_chunk.at[0], recv_chunk.at[k], partner).wait_recv()

        if False:
            @pl.when((dep == 2) | (dep == 7))
            def _():
                for k in range(2):
                    copy(chunks.at[0], far_parts.at[k], send_chunk.at[0], recv_far.at[k], partner).wait_recv()
                far_sum[...] = far_parts[0] + far_parts[1]
                relay_copy().start()

        @pl.when(first)
        def _():
            await_chunk(1 - core)

        @pl.when(jnp.logical_not(first))
        def _():
            await_chunk(0)
            await_chunk(1)

        blank = jnp.zeros((width, width), F32)

        def shifted_right(plane, amount):
            return pltpu.roll(jnp.concatenate([plane, blank], 1), amount, 1)

        def add_up(k):
            grad_copy(k).wait_recv()
            copy(spill_out.at[k], spill_in.at[k], send_spill.at[k], recv_spill.at[k], partner).wait_recv()
            for part in range(2):
                grad[k, part] = (
                    shifted_right(mine[k, part], col_mine)
                    + shifted_right(pair_in[k, part], col_pair)
                    + shifted_right(spill_in[k, part], col_before)
                )

        value = parts[0] + parts[1]
        base = 0
        for level, clique in enumerate(cliques):
            total[level] = value
            hops = [
                copy(
                    total.at[level], around.at[base + k], send_around.at[base + k],
                    recv_around.at[base + k], device,
                )
                for k, device in enumerate(clique)
            ]
            for hop in hops:
                hop.start()
            for k in range(slab):
                if level == len(cliques) - 1:
                    add_up(k)
            for k, hop in enumerate(hops):
                hop.wait_recv()
                value = value + around[base + k]
            base += len(clique)
        probe_grad[...] = value

        note_copy().wait_send()
        for k in range(slab):
            if k < early:
                pl.when(split_core)(lambda: early_copy(k).wait_send())
                pl.when(jnp.logical_not(split_core))(lambda: halo_copy(k).wait_send())
            else:
                halo_copy(k).wait_send()
            pair_copy(k).wait_send()
            grad_copy(k).wait_send()

        @pl.when(last & (core == 1))
        def _():
            seen_copy().wait_send()

        @pl.when(split_core)
        def _():
            for k in range(count):
                spill_copy(k).wait_send()

        @pl.when(jnp.logical_not(last))
        def _():
            wave_copy().wait_send()

        @pl.when(jnp.logical_not(first))
        def _():
            back_copy().wait_send()

        @pl.when(first)
        def _():
            for side in range(2):
                @pl.when(core == side)
                def _():
                    for k in range(depth_count):
                        if k != side:
                            chunk_copy(k, side).wait_send()

        if False:
            @pl.when((dep == 2) | (dep == 7))
            def _():
                relay_copy().wait_send()

        base = 0
        for level, clique in enumerate(cliques):
            for k, device in enumerate(clique):
                copy(
                    total.at[level], around.at[base + k], send_around.at[base + k],
                    recv_around.at[base + k], device,
                ).wait_send()
            base += len(clique)

    links = sum(side - 1 for side in sides)
    share = width // depth_count
    plane = (2, width, width)
    buffers = [
        (slab,) + plane, (slab,) + plane, (count,) + plane, (count,) + plane, (2, 2 * width, width),
        (count,) + plane, (count + 1,) + plane, plane, plane, (count,) + plane, (2, 3 * width, width),
        (slab,) + plane, (slab,) + plane, (slab,) + plane, (count,) + plane, (slab,) + plane,
        (width, width), (width, width), (depth_count, 2, share, width), (2, 2, share, width),
        (len(sides), 2, share, width), (links, 2, share, width),
    ]
    dma = pltpu.SemaphoreType.DMA
    marks = [
        dma((slab,)), dma((slab,)), dma, dma, dma((slab,)), dma((count,)), dma, dma((depth_count,)), dma((links,)),
        dma((count,)), dma((slab,)), dma, dma, dma((slab,)), dma((slab,)), dma, dma((2,)), dma((links,)),
    ]
    square = (2 * width, 2 * width)
    tables = [(6 * width, 2 * width), square, square] * 2
    inputs = [(slab, 2, width, 2 * width), plane, plane]
    head = [pltpu.VMEM(shape, BF16) for shape in tables] + [pltpu.VMEM(shape, F32) for shape in inputs]
    head += [pltpu.SMEM((2,), jnp.int32)] * 4
    head += [dma((6,)), dma((slab,)), dma((4,)), dma, dma]
    piece = (2, share, width)
    head += [pltpu.VMEM((slab, 2, width, 2 * width), F32), dma((slab,))]
    head += [pltpu.VMEM((early, 2, width, 2 * width), F32), pltpu.VMEM((2,) + piece, F32), pltpu.VMEM(piece, F32)]
    head += [dma((2,)), dma]
    return kernel, head + [pltpu.VMEM(shape, F32) for shape in buffers] + marks


def body(objects, probe, row_offsets, col_offsets, intensity):
    slab = objects.shape[0]
    width = probe.shape[-1]
    depth_count = lax.axis_size("depth")
    scan_count = lax.axis_size("scan")
    kernel, scratch = make_kernel(depth_count, scan_count, slab, width)
    tables = [jnp.asarray(table) for table in transfer_tables(width)]
    vmem = pl.BlockSpec(memory_space=pltpu.VMEM)
    anywhere = pl.BlockSpec(memory_space=pl.ANY)
    held = pl.pallas_call(
        kernel,
        out_shape=(
            pltpu.VMEM(objects.shape, F32),
            pltpu.VMEM((2, width // depth_count, width), F32),
        ),
        in_specs=[anywhere] * 11,
        out_specs=(vmem, vmem),
        scratch_shapes=scratch,
        compiler_params=pltpu.CompilerParams(
            collective_id=0, has_side_effects=True, vmem_limit_bytes=56 << 20
        ),
        name="slices",
    )(row_offsets, col_offsets, objects, probe, intensity, *tables)

    def store(grad, probe_grad, grad_hbm, probe_grad_hbm, marks):
        moves = [pltpu.make_async_copy(grad.at[k], grad_hbm.at[k], marks.at[k]) for k in range(slab)]
        moves.append(pltpu.make_async_copy(probe_grad, probe_grad_hbm, marks.at[slab]))
        for move in moves:
            move.start()
        for move in moves:
            move.wait()

    return pl.pallas_call(
        store,
        out_shape=tuple(jax.ShapeDtypeStruct(part.shape, F32) for part in held),
        in_specs=[pl.BlockSpec(memory_space=pltpu.VMEM)] * 2,
        compiler_params=pltpu.CompilerParams(vmem_limit_bytes=1 << 20),
        out_specs=(anywhere, anywhere),
        scratch_shapes=[pltpu.SemaphoreType.DMA((slab + 1,))],
        name="store",
    )(*held)


def solution(mesh):
    in_specs = (P("depth", None, "scan", None), P(), P("scan"), P("scan"), P("scan", None, None))
    out_specs = (P("depth", None, "scan", None), P(None, "depth", None))
    return jax.shard_map(body, mesh=mesh, in_specs=in_specs, out_specs=out_specs, check_vma=False)
```
